32 devices in a mesh: blk: 16 (over z, y, core), dp: 2 (over x).
Axes of the slice: x: 2, y: 2, z: 4, core: 2. Of those that a mesh axis runs over, the one named last changes fastest.
Arguments:
- tokens: bfloat16 [4096, 3584], P(('blk', 'dp')), may hold values from -6 to 6
- route_dir: int32 [4096, 1], P(('blk', 'dp')), may hold values from 0 to 2; in each aligned block of 128 rows (0 to 127, 128 to 255, ...) at most 64 rows name the same one
- gate_probs: float32 [4096, 1], P(('blk', 'dp')), may hold values from 0.3 to 1
- gate_weight: bfloat16 [16, 3584, 512], P('blk', 'dp'), may hold values from -0.09375 to 0.09375
- up_weight: bfloat16 [16, 3584, 512], P('blk', 'dp'), may hold values from -0.09375 to 0.09375
- down_weight: bfloat16 [16, 3584, 512], P('blk', 'dp'), may hold values from -0.1875 to 0.1875
Outputs:
- d_tokens: bfloat16 [4096, 3584], P(('blk', 'dp'))
- grad_gate: bfloat16 [16, 3584, 512], P('blk', 'dp')
- grad_up: bfloat16 [16, 3584, 512], P('blk', 'dp')
- grad_down: bfloat16 [16, 3584, 512], P('blk', 'dp')
The draws below stay inside these ranges and needn't reach their ends.
Inputs may be any that keep to these rules, and one draw needn't show every extreme that they name: A token on blk index b sends its row to expert e = (b // 2 + route_dir - 1) mod 8, whose halves sit at blk indices 2e and 2e + 1; on one device at most 64 tokens take the same value.
All inputs are finite; a program needn't handle non-finite values.
Results may differ from the reference program's by a relative error of at most 0.0079.
Values may be sent and summed in bfloat16 or wider, within the bound.
A program may use at most 128 MiB of HBM per device.

```python
import math
import jax
import jax.numpy as jnp
import numpy as np
from jax import lax

D = 3584
FF = 1024
TOK_DEV = 128
HALF = 512
CAP = 64
EXPERTS = 8
TOKENS = 4096
N_BLK = 16
N_DP = 2


def block_levels(stream_key, dims, split, least, largest):
    factor_of = 1.0
    for position, parts in split:
        draws = jax.random.uniform(jax.random.fold_in(jax.random.fold_in(stream_key, 6), position), (parts,), jnp.float32, least / len(split), largest / len(split))
        factor_of = factor_of * jnp.repeat(jnp.exp(draws), dims[position] // parts).reshape((-1,) + (1,) * (len(dims) - 1 - position))
    return factor_of


def deal_out(key, own, number, rows, number_of, top, bound, skew):
    sequence = jax.random.permutation(key, number_of)
    crowded, ordinary = portions_of(number_of, rows * top, bound, skew, True), portions_of(number_of, rows * top, bound, skew, False)
    places = jnp.arange(number_of)

    def named(sizes, rotation):
        used = int((sizes > 0).sum())
        fixed = max(1, used // 4)
        moved = fixed + (places - fixed + rotation * (used - fixed)) % max(1, number_of - fixed)
        return jnp.zeros((number_of,), jnp.int32).at[sequence[jnp.where(places < fixed, places, moved)]].set(jnp.asarray(sizes, jnp.int32))

    sizes = jnp.where(number % 4 == 0, named(crowded, number // 4), named(ordinary, number - number // 4 - 1))
    mixed = jax.random.permutation(jax.random.fold_in(own, 3), number_of)
    donor, taker = mixed[0:number_of // 2 * 2:2], mixed[1:number_of // 2 * 2:2]
    margin = jnp.minimum(sizes[donor] - 1, bound - sizes[taker]) // 2
    margin = jnp.where((donor == sequence[0]) | (taker == sequence[0]) | (sizes[taker] == 0), 0, jnp.maximum(margin, 0))
    moved = jax.random.randint(jax.random.fold_in(own, 4), (number_of // 2,), 0, 1 << 20) % (margin + 1)
    sizes = sizes.at[donor].add(-moved).at[taker].add(moved)
    labels = jnp.searchsorted(jnp.cumsum(sizes), jnp.arange(rows * top), side="right").astype(jnp.int32)
    listing = labels.reshape(top, rows).T
    listing = listing[jax.random.permutation(jax.random.fold_in(own, 1), rows)]
    rotation = jax.random.randint(jax.random.fold_in(own, 2), (rows, 1), 0, top)
    return jnp.take_along_axis(listing, (jnp.arange(top)[None, :] + rotation) % top, axis=1)


def portions_of(number_of, total, bound, slope, full):
    portions = [(1 << 20) // math.isqrt(rank ** slope) + 1 for rank in range(1, number_of + 1)]
    largest = bound if full else min(bound, max(-(-total // number_of), total * portions[0] // sum(portions)))
    least = 1 if total - largest >= number_of - 1 else 0
    counts, surplus = [largest] + [least] * (number_of - 1), total - largest - least * (number_of - 1)
    while surplus > 0:
        free = [i for i in range(1, number_of) if counts[i] < largest] or [i for i in range(1, number_of) if counts[i] < bound]
        whole, remaining = sum([portions[i] for i in free]), surplus
        for i in free:
            more = min(bound - counts[i], max(1, remaining * portions[i] // whole), surplus)
            counts[i] = counts[i] + more
            surplus = surplus - more
    return np.array(counts)


def centred(stream_key, shape, deviation, bound, shards=(), kind=jnp.bfloat16):
    gain = block_levels(stream_key, shape, shards, -0.22, 0.18) if shards else 1.0
    values = jax.random.normal(stream_key, shape, jnp.float32) * deviation * gain
    return jnp.minimum(jnp.maximum(values, -bound), bound).astype(kind)


def setup_inputs(seed: int = 0) -> dict:
    keys = jax.random.split(jax.random.key(seed), 7)
    tokens = centred(keys[0], (TOKENS, D), 1.0, 6.0, ((0, 32),))
    route_dir_keys = jax.random.split(jax.random.fold_in(keys[1], 1), TOKENS // TOK_DEV)
    route_dir_turns = jax.random.permutation(jax.random.fold_in(keys[1], 3), TOKENS // TOK_DEV)
    route_dir = jax.vmap(lambda own, number: deal_out(jax.random.fold_in(keys[1], 2), own, number, TOK_DEV, 3, 1, CAP, 2))(route_dir_keys, route_dir_turns).reshape((TOKENS, 1))
    gate_probs = jnp.clip(0.3 + 0.7 * jax.random.uniform(keys[2], (TOKENS, 1), jnp.float32) ** block_levels(keys[2], (TOKENS, 1), ((0, 32),), -0.2, 0.2), 0.3, 1.0)
    gate_weight = centred(keys[3], (2 * EXPERTS, D, HALF), D ** -0.5, 0.09375, ((0, 16), (1, 2)))
    up_weight = centred(keys[4], (2 * EXPERTS, D, HALF), D ** -0.5, 0.09375, ((0, 16), (1, 2)))
    down_weight = centred(keys[5], (2 * EXPERTS, D, HALF), FF ** -0.5, 0.1875, ((0, 16), (1, 2)))
    return {"tokens": tokens, "route_dir": route_dir, "gate_probs": gate_probs, "gate_weight": gate_weight, "up_weight": up_weight, "down_weight": down_weight}


def selection(directions, capacity):
    slot_ids = jnp.arange(capacity, dtype=jnp.int32)
    planes = []
    for direction in range(3):
        chosen = (directions == direction).astype(jnp.int32)
        places = jnp.cumsum(chosen, axis=-1, dtype=jnp.int32) - 1
        matches = (chosen[..., None, :] == 1) & (places[..., None, :] == slot_ids[:, None])
        planes.append(matches)
    return jnp.stack(planes, axis=-3).astype(jnp.bfloat16)

def round_trip(payload):
    return lax.optimization_barrier(payload.astype(jnp.bfloat16)).astype(jnp.float32)

def matmul(left_side, right_side):
    return jnp.dot(left_side, right_side, preferred_element_type=jnp.float32)

def times_transposed(left_side, right_side):
    return lax.dot_general(left_side, right_side, (((1,), (1,)), ((), ())), preferred_element_type=jnp.float32)

def activate(pre_gate, pre_up):
    sigmoid = jax.nn.sigmoid(pre_gate)
    return ((pre_gate * sigmoid * pre_up).astype(jnp.bfloat16), sigmoid)

def hidden_grads(d_hidden, pre_gate, pre_up, sigmoid):
    d_gate = (d_hidden * pre_up * (sigmoid * (1.0 + pre_gate * (1.0 - sigmoid)))).astype(jnp.bfloat16)
    d_up = (d_hidden * (pre_gate * sigmoid)).astype(jnp.bfloat16)
    return (d_gate, d_up)

def group_grad(left_side, right_side, groups):
    lhs_float = left_side.reshape(groups, -1, left_side.shape[-1]).astype(jnp.float32)
    rhs_float = right_side.reshape(groups, -1, right_side.shape[-1]).astype(jnp.float32)
    group_terms = jnp.einsum('grk,grh->gkh', lhs_float, rhs_float)
    return lax.optimization_barrier(jnp.sum(round_trip(group_terms), axis=0)).astype(jnp.bfloat16)

def reference(tokens, route_dir, gate_probs, gate_weight, up_weight, down_weight):
    blocks = tokens.reshape(N_BLK, N_DP, TOK_DEV, D)
    directions = route_dir.reshape(N_BLK, N_DP, TOK_DEV)
    weights_in = gate_probs.reshape(N_BLK, N_DP, TOK_DEV)
    selector = selection(directions, CAP)
    offsets = jnp.array([2, 3, 0, 1, -2, -1], dtype=jnp.int32)
    side_ids = jnp.array([0, 0, 1, 1, 2, 2], dtype=jnp.int32)
    row_count = N_DP * 6 * CAP

    def one_expert(expert):
        sources = (offsets + 2 * expert) % N_BLK
        chosen = selector[sources, :, side_ids].astype(jnp.float32)
        gathered = jnp.einsum('ndst,ndtk->ndsk', chosen, blocks[sources].astype(jnp.float32)).astype(jnp.bfloat16)
        scales = jnp.einsum('ndst,ndt->nds', chosen, weights_in[sources])
        inputs = gathered.transpose(1, 0, 2, 3).reshape(row_count, D)
        scales = scales.transpose(1, 0, 2).reshape(row_count, 1)
        stored = []
        partial_sum = jnp.zeros((row_count, D), jnp.float32)
        for which_half in range(2):
            member = 2 * expert + which_half
            w_gate = lax.dynamic_index_in_dim(gate_weight, member, 0, keepdims=False)
            w_up = lax.dynamic_index_in_dim(up_weight, member, 0, keepdims=False)
            w_down = lax.dynamic_index_in_dim(down_weight, member, 0, keepdims=False)
            pre_gate = matmul(inputs, w_gate)
            pre_up = matmul(inputs, w_up)
            activated, sigmoid = activate(pre_gate, pre_up)
            partial_sum = partial_sum + round_trip(times_transposed(activated, w_down))
            stored.append((w_gate, w_up, w_down, pre_gate, pre_up, activated, sigmoid))
        result = scales * round_trip(partial_sum)
        back_rows = (scales * result).astype(jnp.bfloat16)
        grads_gate = []
        grads_up = []
        grads_down = []
        dx_sum = jnp.zeros((row_count, D), jnp.float32)
        for w_gate, w_up, w_down, pre_gate, pre_up, activated, sigmoid in stored:
            d_hidden = matmul(back_rows, w_down)
            d_gate, d_up = hidden_grads(d_hidden, pre_gate, pre_up, sigmoid)
            grads_gate.append(group_grad(inputs, d_gate, N_DP))
            grads_up.append(group_grad(inputs, d_up, N_DP))
            grads_down.append(group_grad(back_rows, activated, N_DP))
            dx_sum = dx_sum + round_trip(times_transposed(d_gate, w_gate) + times_transposed(d_up, w_up))
        dx_rows = dx_sum.astype(jnp.bfloat16).reshape(N_DP, 6, CAP, D).transpose(1, 0, 2, 3)
        return (dx_rows, jnp.stack(grads_gate), jnp.stack(grads_up), jnp.stack(grads_down))
    dx_rows, grads_gate, grads_up, grads_down = lax.map(one_expert, jnp.arange(EXPERTS, dtype=jnp.int32))

    def one_source(source):
        pieces = []
        for direction in range(3):
            expert = (source // 2 + direction - 1) % EXPERTS
            slot_id = 2 * direction + source % 2
            pieces.append(dx_rows[expert, slot_id])
        stacked = jnp.stack(pieces, axis=1)
        return jnp.einsum('djst,djsk->dtk', selector[source].astype(jnp.float32), stacked.astype(jnp.float32)).astype(jnp.bfloat16)
    d_tokens = lax.map(one_source, jnp.arange(N_BLK, dtype=jnp.int32)).reshape(TOKENS, D)
    shape_out = (2 * EXPERTS, D, HALF)
    return (d_tokens, grads_gate.reshape(shape_out), grads_up.reshape(shape_out), grads_down.reshape(shape_out))
```

```python
import functools

import jax
import jax.numpy as jnp
from jax import lax
from jax.experimental import pallas as pl
from jax.experimental.pallas import tpu as pltpu
from jax.sharding import PartitionSpec as P

CAP = 64
TILE = 256
MESH = pl.DeviceIdType.MESH
F32, BF16 = jnp.float32, jnp.bfloat16


def dot(left_side, right_side, left_dim, right_dim):
    return lax.dot_general(
        left_side, right_side, (((left_dim,), (right_dim,)), ((), ())), preferred_element_type=F32
    )


def places_of(chosen):
    tokens = chosen.shape[1]
    before = lax.broadcasted_iota(jnp.int32, (tokens, tokens), 0)
    after = lax.broadcasted_iota(jnp.int32, (tokens, tokens), 1)
    return dot(chosen.astype(BF16), (before <= after).astype(BF16), 1, 0) - 1.0


def slots_of(chosen_row, place_row):
    tokens = chosen_row.shape[1]
    key = jnp.where(chosen_row, place_row, -1.0)
    slot = lax.broadcasted_iota(jnp.int32, (CAP, tokens), 0).astype(F32)
    return slot == jnp.broadcast_to(key, (CAP, tokens))


def kernel(
    n_blk,
    tok, route, probs, w_gate, w_up, w_down,
    out_tok, out_gate, out_up, out_down,
    wg, wu, wd, near_tok, far_tok, facts, sel, outbox, rows,
    pre, pre_send, pre_recv, hid, o_send, o_recv, back, gcol,
    dh, dh_send, dh_recv, dgate, dup, dx_part, dx_recv, dx_sum, home,
    res_near, res_far, grads,
    load_sem, tok_s, tok_r, xf_s, xf_r, ob_s, ob_r, of_s, of_r, side_s, side_r, sf_s, sf_r,
    pre_s, pre_r, o_s, o_r, dh_s, dh_r, dx_s, dx_r, home_s, home_r, res_s, res_r,
    near_sem, grad_sem,
):
    b, d = lax.axis_index("blk"), lax.axis_index("dp")
    c = lax.rem(b, 2)
    other_core = 1 - c
    partner, across = (b + 1 - 2 * c, d), (b, 1 - d)
    upper, lower = (lax.rem(b + 2, n_blk), d), (lax.rem(b + n_blk - 2, n_blk), d)
    wide = near_tok.shape[1]
    hidden = wg.shape[1]
    mine = pl.ds(pl.multiple_of(d * wide, 128), wide)
    theirs = pl.ds(pl.multiple_of((1 - d) * wide, 128), wide)

    def remote(src, dst, ssem, rsem, device):
        return pltpu.make_async_remote_copy(
            src_ref=src, dst_ref=dst, send_sem=ssem, recv_sem=rsem,
            device_id=device, device_id_type=MESH,
        )

    loads = [
        pltpu.make_async_copy(tok.at[:, mine], near_tok, load_sem.at[0]),
        pltpu.make_async_copy(w_gate, wg, load_sem.at[1]),
        pltpu.make_async_copy(w_up, wu, load_sem.at[2]),
        pltpu.make_async_copy(w_down, wd, load_sem.at[3]),
    ]
    for load in loads:
        load.start()

    barrier = pltpu.get_barrier_semaphore()
    for device in (partner, across, upper, lower):
        pl.semaphore_signal(barrier, inc=1, device_id=device, device_id_type=MESH)
    pl.semaphore_wait(barrier, 4)

    x_tok = remote(tok.at[:, theirs], far_tok, tok_s, tok_r, across)
    x_facts = remote(facts.at[0, 1, c], facts.at[1, 1, c], xf_s, xf_r, across)

    def out_rows(g, k):
        return remote(
            outbox.at[g, k], rows.at[g, 2 * k, c], ob_s.at[g, k], ob_r.at[g, k], (lower, upper)[k]
        )

    def out_facts(g, k):
        return remote(
            facts.at[g, 1, c], facts.at[g, 2 * k, c], of_s.at[g, k], of_r.at[g, k],
            (lower, upper)[k],
        )

    def side_rows(g, j):
        return remote(
            rows.at[g, j, c], rows.at[g, j, c], side_s.at[g, j], side_r.at[g, j], partner
        )

    def side_facts(g, j):
        return remote(facts.at[g, j, c], facts.at[g, j, c], sf_s.at[g, j], sf_r.at[g, j], partner)

    def side_rows_in(g, j):
        return remote(
            rows.at[g, j, other_core], rows.at[g, j, other_core],
            side_s.at[g, j], side_r.at[g, j], partner,
        )

    def side_facts_in(g, j):
        return remote(
            facts.at[g, j, other_core], facts.at[g, j, other_core],
            sf_s.at[g, j], sf_r.at[g, j], partner,
        )

    def x_pre(g, j):
        return remote(
            pre_send.at[g, j], pre_recv.at[1 - g, j], pre_s.at[g, j], pre_r.at[1 - g, j], across
        )

    def o_copy(g, j):
        return remote(o_send.at[g, j], o_recv.at[g, j], o_s.at[g, j], o_r.at[g, j], partner)

    def x_dh(g, j):
        return remote(
            dh_send.at[g, j], dh_recv.at[1 - g, j], dh_s.at[g, j], dh_r.at[1 - g, j], across
        )

    def dx_copy(g, j):
        return remote(
            dx_part.at[g, j, other_core], dx_recv.at[g, j], dx_s.at[g, j], dx_r.at[g, j], partner
        )

    def home_copy(g, k):
        return remote(
            dx_sum.at[g, 2 * k], home.at[g, 2 * k], home_s.at[g, k], home_r.at[g, k],
            (upper, lower)[k],
        )

    x_res = remote(res_far, out_tok.at[:, mine], res_s, res_r, across)

    def choose(g):
        fact = facts[g, 1, c]
        kinds = lax.broadcasted_iota(jnp.int32, fact.shape, 0).astype(F32)
        chosen = jnp.broadcast_to(fact[0:1], fact.shape) == kinds
        place = places_of(chosen.astype(F32))
        kept = jnp.where(chosen, place, -1.0)
        slot = lax.broadcasted_iota(jnp.int32, (CAP, fact.shape[1]), 0).astype(F32)
        for j in range(3):
            key = jnp.broadcast_to(kept[j : j + 1], (CAP, fact.shape[1]))
            sel[g, j] = (slot == key).astype(F32).astype(BF16)

    def pick(g, j, source, target):
        target[...] = dot(sel[g, j], source[...], 1, 0).astype(BF16)

    def front(g, source):
        choose(g)
        pick(g, 0, source, outbox.at[g, 0])
        out_rows(g, 0).start()
        pick(g, 2, source, outbox.at[g, 1])
        out_rows(g, 1).start()
        pick(g, 1, source, rows.at[g, 1, c])
        side_rows(g, 1).start()
        for k in range(2):
            out_facts(g, k).start()
        side_facts(g, 1).start()

    x_tok.start()
    pad = jnp.zeros((facts.shape[3] - 2, facts.shape[4]), F32)
    facts[0, 1, c] = jnp.concatenate([route[...].astype(F32), probs[...], pad], axis=0)
    x_facts.start()
    loads[0].wait()
    front(0, near_tok)
    loads[1].wait()
    loads[2].wait()

    @pl.loop(0, 6)
    def _(u):
        g, i = u // 3, u % 3
        j = (1 + 2 * i) % 3

        @pl.when(u == 1)
        def _():
            x_facts.wait_recv()
            x_tok.wait_recv()
            front(1, far_tok)

        @pl.when(i == 1)
        def _():
            for k in range(2):
                out_rows(g, k).wait_recv()
                side_rows(g, 2 * k).start()
            for k in range(2):
                out_facts(g, k).wait_recv()
                side_facts(g, 2 * k).start()

        side_rows_in(g, j).wait_recv()
        unit = rows[g, j].reshape(2 * CAP, wide)
        for part, weight in enumerate((wg, wu)):
            cols = pl.ds(part * hidden, hidden)
            value = dot(unit, weight[...], 1, 0)
            pre[g, j, :, cols] = value
            pre_send[g, j, :, cols] = value.astype(BF16)

        @pl.when(g == 0)
        def _():
            x_pre(g, j).start()

        @pl.when(u == 4)
        def _():
            x_pre(1, 0).start()

        @pl.when(u == 5)
        def _():
            x_pre(1, 2).start()
            x_pre(1, 1).start()

    loads[3].wait()

    def activate(g, j):
        x_pre(1 - g, j).wait_recv()
        full = pre[g, j] + pre_recv[g, j].astype(F32)
        pre[g, j] = full
        gate, up = full[:, :hidden], full[:, hidden:]
        act = (gate * jax.nn.sigmoid(gate) * up).astype(BF16)
        hid[g, j] = act
        o_send[g, j] = dot(act, wd[...], 1, 1).astype(BF16)
        o_copy(g, j).start()

    def back_unit(g, j):
        side_facts_in(g, j).wait_recv()
        for s in range(2):
            fact = facts[g, j, s]
            chosen = jnp.broadcast_to(fact[0:1], fact.shape) == j.astype(F32)
            place = places_of(chosen.astype(F32))
            slots = slots_of(chosen[0:1], place[0:1])
            weight = jnp.where(slots, jnp.broadcast_to(fact[1:2], slots.shape), 0.0)
            gcol[g, j, s] = jnp.broadcast_to(
                jnp.sum(weight, axis=1, keepdims=True), gcol.shape[3:]
            )
        o_copy(g, j).wait_recv()
        gates = gcol[g, j].reshape(2 * CAP, gcol.shape[4])[:, 0:1]
        total = (o_send[g, j].astype(F32) + o_recv[g, j].astype(F32)).astype(BF16)
        rows_back = (gates * (gates * total.astype(F32))).astype(BF16)
        back[g, j] = rows_back
        value = dot(rows_back, wd[...], 1, 0)
        dh[g, j] = value
        dh_send[g, j] = value.astype(BF16)

        @pl.when(g == 0)
        def _():
            x_dh(g, j).start()

    def unit_of(t):
        g = 1 - t // 3
        return g, (2 * (t % 3) + g) % 3

    @pl.loop(0, 7)
    def _(t):
        @pl.when(t < 3)
        def _():
            activate(*unit_of(t))

        @pl.when(t > 0)
        def _():
            back_unit(*unit_of(t - 1))

        @pl.when((t > 2) & (t < 6))
        def _():
            activate(*unit_of(t))

    for j in (0, 2, 1):
        x_dh(1, j).start()

    def grad_unit(k, left, right, target):
        @pl.loop(0, wide // TILE)
        def _(n):
            cols = pl.ds(pl.multiple_of(n * TILE, TILE), TILE)
            value = dot(
                left[..., cols].reshape(-1, TILE), right[...].reshape(-1, hidden), 0, 0
            )
            grads[k, cols, :] = value.astype(BF16)
            pltpu.make_async_copy(
                grads.at[k, cols, :], target.at[cols, :], grad_sem.at[k, n]
            ).start()

    def down_unit(g, j):
        x_dh(1 - g, j).wait_recv()
        d_hidden = dh[g, j] + dh_recv[g, j].astype(F32)
        gate, up = pre[g, j, :, :hidden], pre[g, j, :, hidden:]
        sigmoid = jax.nn.sigmoid(gate)
        d_g = (d_hidden * up * (sigmoid * (1.0 + gate * (1.0 - sigmoid)))).astype(BF16)
        d_u = (d_hidden * (gate * sigmoid)).astype(BF16)
        dgate[g, j] = d_g
        dup[g, j] = d_u
        value = dot(d_g, wg[...], 1, 1) + dot(d_u, wu[...], 1, 1)
        dx_part[g, j] = value.astype(BF16).reshape(2, CAP, wide)
        dx_copy(g, j).start()

    def join_unit(g, j):
        dx_copy(g, j).wait_recv()
        dx_sum[g, j] = (dx_part[g, j, c].astype(F32) + dx_recv[g, j].astype(F32)).astype(BF16)

        @pl.when(j == 0)
        def _():
            home_copy(g, 0).start()

        @pl.when(j == 2)
        def _():
            home_copy(g, 1).start()

        @pl.when(j == 1)
        def _():
            home[g, j] = dx_sum[g, j]

    def unpack(g, target):
        for k in range(2):
            home_copy(g, k).wait_recv()
        tokens = sel.shape[3]
        target[...] = dot(
            sel[g].reshape(3 * CAP, tokens), home[g].reshape(3 * CAP, wide), 0, 0
        ).astype(BF16)

    def last_of(t):
        return 1 - t // 3, (2 * (t % 3)) % 3

    @pl.loop(0, 7)
    def _(t):
        @pl.when(t > 0)
        def _():
            join_unit(*last_of(t - 1))

        @pl.when(t == 3)
        def _():
            grad_unit(2, back, hid, out_down)

        @pl.when(t == 4)
        def _():
            unpack(1, res_far)
            x_res.start()

        @pl.when(t < 6)
        def _():
            down_unit(*last_of(t))

    grad_unit(0, rows, dgate, out_gate)
    grad_unit(1, rows, dup, out_up)
    unpack(0, res_near)
    near_out = pltpu.make_async_copy(res_near, out_tok.at[:, mine], near_sem)
    near_out.start()

    x_tok.wait_send()
    x_facts.wait_send()
    for g in range(2):
        for k in range(2):
            out_rows(g, k).wait_send()
            out_facts(g, k).wait_send()
            home_copy(g, k).wait_send()
        for j in range(3):
            side_rows(g, j).wait_send()
            side_facts(g, j).wait_send()
            x_pre(g, j).wait_send()
            o_copy(g, j).wait_send()
            x_dh(g, j).wait_send()
            dx_copy(g, j).wait_send()
    for k, target in enumerate((out_gate, out_up, out_down)):
        for n in range(wide // TILE):
            cols = pl.ds(n * TILE, TILE)
            pltpu.make_async_copy(
                grads.at[k, cols, :], target.at[cols, :], grad_sem.at[k, n]
            ).wait()
    near_out.wait()
    x_res.wait_send()
    remote(res_far, out_tok.at[:, theirs], res_s, res_r, across).wait_recv()


def per_device(n_blk, tokens, route_dir, gate_probs, gate_weight, up_weight, down_weight):
    count, model = tokens.shape
    _, wide, hidden = gate_weight.shape
    dma = pltpu.SemaphoreType.DMA
    vmem = pltpu.VMEM
    units = 2 * CAP
    outs = pl.pallas_call(
        functools.partial(kernel, n_blk),
        out_shape=(
            jax.ShapeDtypeStruct((count, model), BF16),
            jax.ShapeDtypeStruct((wide, hidden), BF16),
            jax.ShapeDtypeStruct((wide, hidden), BF16),
            jax.ShapeDtypeStruct((wide, hidden), BF16),
        ),
        in_specs=[
            pl.BlockSpec(memory_space=pl.ANY),
            pl.BlockSpec(memory_space=pltpu.VMEM),
            pl.BlockSpec(memory_space=pltpu.VMEM),
            pl.BlockSpec(memory_space=pl.ANY),
            pl.BlockSpec(memory_space=pl.ANY),
            pl.BlockSpec(memory_space=pl.ANY),
        ],
        out_specs=[pl.BlockSpec(memory_space=pl.ANY)] * 4,
        scratch_shapes=[
            vmem((wide, hidden), BF16),
            vmem((wide, hidden), BF16),
            vmem((wide, hidden), BF16),
            vmem((count, wide), BF16),
            vmem((count, wide), BF16),
            vmem((2, 3, 2, 8, count), F32),
            vmem((2, 3, CAP, count), BF16),
            vmem((2, 2, CAP, wide), BF16),
            vmem((2, 3, 2, CAP, wide), BF16),
            vmem((2, 3, units, 2 * hidden), F32),
            vmem((2, 3, units, 2 * hidden), BF16),
            vmem((2, 3, units, 2 * hidden), BF16),
            vmem((2, 3, units, hidden), BF16),
            vmem((2, 3, units, wide), BF16),
            vmem((2, 3, units, wide), BF16),
            vmem((2, 3, units, wide), BF16),
            vmem((2, 3, 2, CAP, 128), F32),
            vmem((2, 3, units, hidden), F32),
            vmem((2, 3, units, hidden), BF16),
            vmem((2, 3, units, hidden), BF16),
            vmem((2, 3, units, hidden), BF16),
            vmem((2, 3, units, hidden), BF16),
            vmem((2, 3, 2, CAP, wide), BF16),
            vmem((2, 3, CAP, wide), BF16),
            vmem((2, 3, CAP, wide), BF16),
            vmem((2, 3, CAP, wide), BF16),
            vmem((count, wide), BF16),
            vmem((count, wide), BF16),
            vmem((3, wide, hidden), BF16),
            dma((4,)),
            dma, dma, dma, dma,
            dma((2, 2)), dma((2, 2)), dma((2, 2)), dma((2, 2)),
            dma((2, 3)), dma((2, 3)), dma((2, 3)), dma((2, 3)),
            dma((2, 3)), dma((2, 3)), dma((2, 3)), dma((2, 3)),
            dma((2, 3)), dma((2, 3)), dma((2, 3)), dma((2, 3)),
            dma((2, 2)), dma((2, 2)),
            dma, dma,
            dma,
            dma((3, wide // TILE)),
        ],
        compiler_params=pltpu.CompilerParams(
            collective_id=0, has_side_effects=True, vmem_limit_bytes=60 << 20
        ),
    )(
        tokens,
        route_dir.reshape(1, count),
        gate_probs.reshape(1, count),
        gate_weight[0],
        up_weight[0],
        down_weight[0],
    )
    d_tokens, grad_gate, grad_up, grad_down = outs
    return d_tokens, grad_gate[None], grad_up[None], grad_down[None]


def solution(mesh):
    return jax.shard_map(
        functools.partial(per_device, mesh.shape["blk"]),
        mesh=mesh,
        in_specs=(
            P(("blk", "dp"), None),
            P(("blk", "dp"), None),
            P(("blk", "dp"), None),
            P("blk", "dp", None),
            P("blk", "dp", None),
            P("blk", "dp", None),
        ),
        out_specs=(
            P(("blk", "dp"), None),
            P("blk", "dp", None),
            P("blk", "dp", None),
            P("blk", "dp", None),
        ),
        check_vma=False,
    )
```

```python
import functools

import jax
import jax.numpy as jnp
from jax import lax
from jax.experimental import pallas as pl
from jax.experimental.pallas import tpu as pltpu
from jax.sharding import PartitionSpec as P

CAP = 64
GRAD_PARTS = 2
MESH = pl.DeviceIdType.MESH
F32, BF16 = jnp.float32, jnp.bfloat16


def dot(left_side, right_side, left_dim, right_dim):
    return lax.dot_general(
        left_side, right_side, (((left_dim,), (right_dim,)), ((), ())), preferred_element_type=F32
    )


def places_of(chosen):
    tokens = chosen.shape[1]
    before = lax.broadcasted_iota(jnp.int32, (tokens, tokens), 0)
    after = lax.broadcasted_iota(jnp.int32, (tokens, tokens), 1)
    return dot(chosen.astype(BF16), (before <= after).astype(BF16), 1, 0) - 1.0


def slots_of(chosen_row, place_row):
    tokens = chosen_row.shape[1]
    key = jnp.where(chosen_row, place_row, -1.0)
    slot = lax.broadcasted_iota(jnp.int32, (CAP, tokens), 0).astype(F32)
    return slot == jnp.broadcast_to(key, (CAP, tokens))


def kernel(
    n_blk,
    tok, route_in, probs_in, w_gate, w_up, w_down,
    out_tok, out_gate, out_up, out_down,
    route, probs, wg, wu, wd, near_tok, far_tok, facts, sel, outbox, rows,
    pre, pre_send, pre_recv, hid, o_send, o_recv, back, gcol,
    dh, dh_send, dh_recv, dgate, dup, dx_part, dx_recv, dx_sum, home,
    res_near, res_far, grads,
    load_sem, tok_s, tok_r, xf_s, xf_r, ob_s, ob_r, of_s, of_r, side_s, side_r, sf_s, sf_r,
    pre_s, pre_r, o_s, o_r, dh_s, dh_r, dx_s, dx_r, home_s, home_r, res_s, res_r,
    near_sem, grad_sem,
):
    b, d = lax.axis_index("blk"), lax.axis_index("dp")
    c = lax.rem(b, 2)
    other_core = 1 - c
    partner, across = (b + 1 - 2 * c, d), (b, 1 - d)
    upper, lower = (lax.rem(b + 2, n_blk), d), (lax.rem(b + n_blk - 2, n_blk), d)
    wide = near_tok.shape[1]
    hidden = wg.shape[1]
    tile = wide // GRAD_PARTS
    mine = pl.ds(pl.multiple_of(d * wide, 128), wide)
    theirs = pl.ds(pl.multiple_of((1 - d) * wide, 128), wide)

    def remote(src, dst, ssem, rsem, device):
        return pltpu.make_async_remote_copy(
            src_ref=src, dst_ref=dst, send_sem=ssem, recv_sem=rsem,
            device_id=device, device_id_type=MESH,
        )

    loads = [
        pltpu.make_async_copy(route_in, route, load_sem.at[4]),
        pltpu.make_async_copy(probs_in, probs, load_sem.at[5]),
        pltpu.make_async_copy(tok.at[:, mine], near_tok, load_sem.at[0]),
        pltpu.make_async_copy(w_gate, wg, load_sem.at[1]),
        pltpu.make_async_copy(w_up, wu, load_sem.at[2]),
        pltpu.make_async_copy(w_down, wd, load_sem.at[3]),
    ]
    for load in loads:
        load.start()

    barrier = pltpu.get_barrier_semaphore()
    for device in (partner, across, upper, lower):
        pl.semaphore_signal(barrier, inc=1, device_id=device, device_id_type=MESH)
    pl.semaphore_wait(barrier, 4)

    x_tok = remote(tok.at[:, theirs], far_tok, tok_s, tok_r, across)
    x_facts = remote(facts.at[0, 1, c], facts.at[1, 1, c], xf_s, xf_r, across)

    def out_rows(g, k):
        return remote(
            outbox.at[g, k], rows.at[g, 2 * k, c], ob_s.at[g, k], ob_r.at[g, k], (lower, upper)[k]
        )

    def out_facts(g, k):
        return remote(
            facts.at[g, 1, c], facts.at[g, 2 * k, c], of_s.at[g, k], of_r.at[g, k],
            (lower, upper)[k],
        )

    def side_rows(g, j):
        return remote(
            rows.at[g, j, c], rows.at[g, j, c], side_s.at[g, j], side_r.at[g, j], partner
        )

    def side_facts(g, j):
        return remote(facts.at[g, j, c], facts.at[g, j, c], sf_s.at[g, j], sf_r.at[g, j], partner)

    def side_rows_in(g, j):
        return remote(
            rows.at[g, j, other_core], rows.at[g, j, other_core],
            side_s.at[g, j], side_r.at[g, j], partner,
        )

    def side_facts_in(g, j):
        return remote(
            facts.at[g, j, other_core], facts.at[g, j, other_core],
            sf_s.at[g, j], sf_r.at[g, j], partner,
        )

    def x_pre(g, j):
        return remote(
            pre_send.at[g, j], pre_recv.at[1 - g, j], pre_s.at[g, j], pre_r.at[1 - g, j], across
        )

    def o_copy(g, j):
        return remote(o_send.at[g, j], o_recv.at[g, j], o_s.at[g, j], o_r.at[g, j], partner)

    def x_dh(g, j):
        return remote(
            dh_send.at[g, j], dh_recv.at[1 - g, j], dh_s.at[g, j], dh_r.at[1 - g, j], across
        )

    def dx_copy(g, j):
        return remote(
            dx_part.at[g, j, other_core], dx_recv.at[g, j], dx_s.at[g, j], dx_r.at[g, j], partner
        )

    def home_copy(g, k):
        return remote(
            dx_sum.at[g, 2 * k], home.at[g, 2 * k], home_s.at[g, k], home_r.at[g, k],
            (upper, lower)[k],
        )

    x_res = remote(res_far, out_tok.at[:, mine], res_s, res_r, across)

    def choose(g):
        fact = facts[g, 1, c]
        kinds = lax.broadcasted_iota(jnp.int32, fact.shape, 0).astype(F32)
        chosen = jnp.broadcast_to(fact[0:1], fact.shape) == kinds
        place = places_of(chosen.astype(F32))
        kept = jnp.where(chosen, place, -1.0)
        slot = lax.broadcasted_iota(jnp.int32, (CAP, fact.shape[1]), 0).astype(F32)
        for j in range(3):
            key = jnp.broadcast_to(kept[j : j + 1], (CAP, fact.shape[1]))
            sel[g, j] = (slot == key).astype(F32).astype(BF16)

    def pick(g, j, source, target):
        target[...] = dot(sel[g, j], source[...], 1, 0).astype(BF16)

    def front(g, source):
        choose(g)
        pick(g, 0, source, outbox.at[g, 0])
        out_rows(g, 0).start()
        pick(g, 2, source, outbox.at[g, 1])
        out_rows(g, 1).start()
        pick(g, 1, source, rows.at[g, 1, c])
        side_rows(g, 1).start()
        for k in range(2):
            out_facts(g, k).start()
        side_facts(g, 1).start()

    x_tok.start()
    pad = jnp.zeros((facts.shape[3] - 2, facts.shape[4]), F32)
    loads[0].wait()
    loads[1].wait()
    facts[0, 1, c] = jnp.concatenate([route[...].astype(F32), probs[...], pad], axis=0)
    x_facts.start()
    loads[2].wait()
    front(0, near_tok)
    loads[3].wait()
    loads[4].wait()

    def forward(g, k):
        out_rows(g, k).wait_recv()
        side_rows(g, 2 * k).start()
        out_facts(g, k).wait_recv()
        side_facts(g, 2 * k).start()

    def first(g, j):
        side_rows_in(g, j).wait_recv()
        unit = rows[g, j].reshape(2 * CAP, wide)
        for part, weight in enumerate((wg, wu)):
            cols = pl.ds(part * hidden, hidden)
            value = dot(unit, weight[...], 1, 0)
            pre[g, j, :, cols] = value
            pre_send[g, j, :, cols] = value.astype(BF16)

    def activate(g, j):
        x_pre(1 - g, j).wait_recv()
        full = pre[g, j] + pre_recv[g, j].astype(F32)
        pre[g, j] = full
        gate, up = full[:, :hidden], full[:, hidden:]
        act = (gate * jax.nn.sigmoid(gate) * up).astype(BF16)
        hid[g, j] = act
        o_send[g, j] = dot(act, wd[...], 1, 1).astype(BF16)
        o_copy(g, j).start()

    def back_unit(g, j):
        side_facts_in(g, j).wait_recv()
        for s in range(2):
            fact = facts[g, j, s]
            chosen = jnp.broadcast_to(fact[0:1], fact.shape) == float(j)
            place = places_of(chosen.astype(F32))
            slots = slots_of(chosen[0:1], place[0:1])
            weight = jnp.where(slots, jnp.broadcast_to(fact[1:2], slots.shape), 0.0)
            gcol[g, j, s] = jnp.broadcast_to(
                jnp.sum(weight, axis=1, keepdims=True), gcol.shape[3:]
            )
        o_copy(g, j).wait_recv()
        gates = gcol[g, j].reshape(2 * CAP, gcol.shape[4])[:, 0:1]
        total = (o_send[g, j].astype(F32) + o_recv[g, j].astype(F32)).astype(BF16)
        rows_back = (gates * (gates * total.astype(F32))).astype(BF16)
        back[g, j] = rows_back
        value = dot(rows_back, wd[...], 1, 0)
        dh[g, j] = value
        dh_send[g, j] = value.astype(BF16)

    def grad_unit(k, left, right, target):
        for n in range(wide // tile):
            cols = pl.ds(n * tile, tile)
            value = dot(
                left[..., cols].reshape(-1, tile), right[...].reshape(-1, hidden), 0, 0
            )
            grads[k, cols, :] = value.astype(BF16)
            pltpu.make_async_copy(
                grads.at[k, cols, :], target.at[cols, :], grad_sem.at[k, n]
            ).start()

    def down_unit(g, j):
        x_dh(1 - g, j).wait_recv()
        d_hidden = dh[g, j] + dh_recv[g, j].astype(F32)
        gate, up = pre[g, j, :, :hidden], pre[g, j, :, hidden:]
        sigmoid = jax.nn.sigmoid(gate)
        d_g = (d_hidden * up * (sigmoid * (1.0 + gate * (1.0 - sigmoid)))).astype(BF16)
        d_u = (d_hidden * (gate * sigmoid)).astype(BF16)
        dgate[g, j] = d_g
        dup[g, j] = d_u
        value = dot(d_g, wg[...], 1, 1) + dot(d_u, wu[...], 1, 1)
        dx_part[g, j] = value.astype(BF16).reshape(2, CAP, wide)
        dx_copy(g, j).start()

    def join_unit(g, j):
        dx_copy(g, j).wait_recv()
        dx_sum[g, j] = (dx_part[g, j, c].astype(F32) + dx_recv[g, j].astype(F32)).astype(BF16)

        if j == 1:
            home[g, j] = dx_sum[g, j]
        else:
            home_copy(g, j // 2).start()

    def unpack(g, target):
        for k in range(2):
            home_copy(g, k).wait_recv()
        tokens = sel.shape[3]
        target[...] = dot(
            sel[g].reshape(3 * CAP, tokens), home[g].reshape(3 * CAP, wide), 0, 0
        ).astype(BF16)

    first(0, 1)
    x_pre(0, 1).start()
    x_facts.wait_recv()
    x_tok.wait_recv()
    front(1, far_tok)
    for k in range(2):
        forward(0, k)
    for j in (0, 2):
        first(0, j)
        x_pre(0, j).start()
    first(1, 1)
    for k in range(2):
        forward(1, k)
    for j in (0, 2):
        first(1, j)
        x_pre(1, j).start()
    loads[5].wait()

    activate(1, 1)
    activate(1, 0)
    back_unit(1, 1)
    activate(1, 2)
    back_unit(1, 0)
    back_unit(1, 2)

    activate(0, 0)
    back_unit(0, 0)
    x_dh(0, 0).start()
    x_pre(1, 1).start()
    activate(0, 2)
    back_unit(0, 2)
    x_dh(0, 2).start()
    x_dh(1, 0).start()
    x_dh(1, 2).start()
    down_unit(1, 0)
    join_unit(1, 0)
    activate(0, 1)
    back_unit(0, 1)
    x_dh(0, 1).start()
    x_dh(1, 1).start()
    down_unit(1, 2)
    join_unit(1, 2)
    down_unit(0, 0)
    down_unit(1, 1)
    join_unit(0, 0)
    join_unit(1, 1)
    unpack(1, res_far)
    x_res.start()
    down_unit(0, 2)
    down_unit(0, 1)
    join_unit(0, 2)
    join_unit(0, 1)
    grad_unit(2, back, hid, out_down)
    grad_unit(0, rows, dgate, out_gate)
    grad_unit(1, rows, dup, out_up)
    unpack(0, res_near)
    near_out = pltpu.make_async_copy(res_near, out_tok.at[:, mine], near_sem)
    near_out.start()

    x_tok.wait_send()
    x_facts.wait_send()
    for g in range(2):
        for k in range(2):
            out_rows(g, k).wait_send()
            out_facts(g, k).wait_send()
            home_copy(g, k).wait_send()
        for j in range(3):
            side_rows(g, j).wait_send()
            side_facts(g, j).wait_send()
            x_pre(g, j).wait_send()
            o_copy(g, j).wait_send()
            x_dh(g, j).wait_send()
            dx_copy(g, j).wait_send()
    for k, target in enumerate((out_gate, out_up, out_down)):
        for n in range(wide // tile):
            cols = pl.ds(n * tile, tile)
            pltpu.make_async_copy(
                grads.at[k, cols, :], target.at[cols, :], grad_sem.at[k, n]
            ).wait()
    near_out.wait()
    x_res.wait_send()
    remote(res_far, out_tok.at[:, theirs], res_s, res_r, across).wait_recv()


def settle_kernel(parts, *refs):
    count = len(refs) // 2
    sources, targets, sem = refs[:count], refs[count : 2 * count], refs[-1]
    copies = []
    for k in range(count):
        rows = sources[k].shape[0] // parts
        for part in range(parts):
            span = pl.ds(part * rows, rows)
            copies.append(
                pltpu.make_async_copy(
                    sources[k].at[span, :], targets[k].at[span, :], sem.at[k, part]
                )
            )
    for copy in copies:
        copy.start()
    for copy in copies:
        copy.wait()


def settled(arrays, parts=4):
    return pl.pallas_call(
        functools.partial(settle_kernel, parts),
        out_shape=tuple(jax.ShapeDtypeStruct(a.shape, a.dtype) for a in arrays),
        in_specs=[pl.BlockSpec(memory_space=pl.ANY)] * len(arrays),
        out_specs=[pl.BlockSpec(memory_space=pltpu.HBM)] * len(arrays),
        scratch_shapes=[pltpu.SemaphoreType.DMA((len(arrays), parts))],
        compiler_params=pltpu.CompilerParams(vmem_limit_bytes=1 << 20),
    )(*arrays)


def in_hbm(array):
    return pltpu.with_memory_space_constraint(array, pltpu.HBM)


def per_device(n_blk, tokens, route_dir, gate_probs, gate_weight, up_weight, down_weight):
    count, model = tokens.shape
    _, wide, hidden = gate_weight.shape
    dma = pltpu.SemaphoreType.DMA
    vmem = pltpu.VMEM
    units = 2 * CAP
    outs = pl.pallas_call(
        functools.partial(kernel, n_blk),
        out_shape=(
            jax.ShapeDtypeStruct((count, model), BF16),
            jax.ShapeDtypeStruct((wide, hidden), BF16),
            jax.ShapeDtypeStruct((wide, hidden), BF16),
            jax.ShapeDtypeStruct((wide, hidden), BF16),
        ),
        in_specs=[
            pl.BlockSpec(memory_space=pltpu.HBM),
            pl.BlockSpec(memory_space=pltpu.HBM),
            pl.BlockSpec(memory_space=pltpu.HBM),
            pl.BlockSpec(memory_space=pltpu.HBM),
            pl.BlockSpec(memory_space=pltpu.HBM),
            pl.BlockSpec(memory_space=pltpu.HBM),
        ],
        out_specs=[pl.BlockSpec(memory_space=pl.ANY)] * 4,
        scratch_shapes=[
            vmem((1, count), jnp.int32),
            vmem((1, count), F32),
            vmem((wide, hidden), BF16),
            vmem((wide, hidden), BF16),
            vmem((wide, hidden), BF16),
            vmem((count, wide), BF16),
            vmem((count, wide), BF16),
            vmem((2, 3, 2, 8, count), F32),
            vmem((2, 3, CAP, count), BF16),
            vmem((2, 2, CAP, wide), BF16),
            vmem((2, 3, 2, CAP, wide), BF16),
            vmem((2, 3, units, 2 * hidden), F32),
            vmem((2, 3, units, 2 * hidden), BF16),
            vmem((2, 3, units, 2 * hidden), BF16),
            vmem((2, 3, units, hidden), BF16),
            vmem((2, 3, units, wide), BF16),
            vmem((2, 3, units, wide), BF16),
            vmem((2, 3, units, wide), BF16),
            vmem((2, 3, 2, CAP, 128), F32),
            vmem((2, 3, units, hidden), F32),
            vmem((2, 3, units, hidden), BF16),
            vmem((2, 3, units, hidden), BF16),
            vmem((2, 3, units, hidden), BF16),
            vmem((2, 3, units, hidden), BF16),
            vmem((2, 3, 2, CAP, wide), BF16),
            vmem((2, 3, CAP, wide), BF16),
            vmem((2, 3, CAP, wide), BF16),
            vmem((2, 3, CAP, wide), BF16),
            vmem((count, wide), BF16),
            vmem((count, wide), BF16),
            vmem((3, wide, hidden), BF16),
            dma((6,)),
            dma, dma, dma, dma,
            dma((2, 2)), dma((2, 2)), dma((2, 2)), dma((2, 2)),
            dma((2, 3)), dma((2, 3)), dma((2, 3)), dma((2, 3)),
            dma((2, 3)), dma((2, 3)), dma((2, 3)), dma((2, 3)),
            dma((2, 3)), dma((2, 3)), dma((2, 3)), dma((2, 3)),
            dma((2, 2)), dma((2, 2)),
            dma, dma,
            dma,
            dma((3, GRAD_PARTS)),
        ],
        compiler_params=pltpu.CompilerParams(
            collective_id=0, has_side_effects=True, vmem_limit_bytes=46 << 20
        ),
    )(
        in_hbm(tokens),
        in_hbm(route_dir.reshape(1, count)),
        in_hbm(gate_probs.reshape(1, count)),
        in_hbm(gate_weight[0]),
        in_hbm(up_weight[0]),
        in_hbm(down_weight[0]),
    )
    d_tokens, grad_gate, grad_up, grad_down = settled(outs)
    return d_tokens, grad_gate[None], grad_up[None], grad_down[None]


def solution(mesh):
    return jax.shard_map(
        functools.partial(per_device, mesh.shape["blk"]),
        mesh=mesh,
        in_specs=(
            P(("blk", "dp"), None),
            P(("blk", "dp"), None),
            P(("blk", "dp"), None),
            P("blk", "dp", None),
            P("blk", "dp", None),
            P("blk", "dp", None),
        ),
        out_specs=(
            P(("blk", "dp"), None),
            P("blk", "dp", None),
            P("blk", "dp", None),
            P("blk", "dp", None),
        ),
        check_vma=False,
    )
```

```python
import functools

import jax
import jax.numpy as jnp
from jax import lax
from jax.experimental import pallas as pl
from jax.experimental.pallas import tpu as pltpu
from jax.sharding import PartitionSpec as P

CAP = 64
GRAD_PARTS = 2
MESH = pl.DeviceIdType.MESH
F32, BF16 = jnp.float32, jnp.bfloat16


def dot(left_side, right_side, left_dim, right_dim):
    return lax.dot_general(
        left_side, right_side, (((left_dim,), (right_dim,)), ((), ())), preferred_element_type=F32
    )


def places_of(chosen):
    tokens = chosen.shape[1]
    before = lax.broadcasted_iota(jnp.int32, (tokens, tokens), 0)
    after = lax.broadcasted_iota(jnp.int32, (tokens, tokens), 1)
    return dot(chosen.astype(BF16), (before <= after).astype(BF16), 1, 0) - 1.0


def slots_of(chosen_row, place_row):
    tokens = chosen_row.shape[1]
    key = jnp.where(chosen_row, place_row, -1.0)
    slot = lax.broadcasted_iota(jnp.int32, (CAP, tokens), 0).astype(F32)
    return slot == jnp.broadcast_to(key, (CAP, tokens))


def kernel(
    n_blk,
    tok, route_in, probs_in, w_gate, w_up, w_down,
    out_tok, out_gate, out_up, out_down,
    route, probs, wg, wu, wd, near_tok, far_tok, facts, sel, outbox, rows,
    pre, pre_send, pre_recv, hid, o_send, o_recv, back, gcol,
    dh, dh_send, dh_recv, dgate, dup, dx_part, dx_recv, dx_sum, home,
    res_near, res_far, grads,
    load_sem, tok_s, tok_r, xf_s, xf_r, ob_s, ob_r, of_s, of_r, side_s, side_r, sf_s, sf_r,
    pre_s, pre_r, o_s, o_r, dh_s, dh_r, dx_s, dx_r, home_s, home_r, res_s, res_r,
    near_sem, grad_sem, across_in, cycle_in,
):
    b, d = lax.axis_index("blk"), lax.axis_index("dp")
    c = lax.rem(b, 2)
    other_core = 1 - c
    partner, across = (b + 1 - 2 * c, d), (b, 1 - d)
    upper, lower = (lax.rem(b + 2, n_blk), d), (lax.rem(b + n_blk - 2, n_blk), d)
    wide = near_tok.shape[1]
    hidden = wg.shape[1]
    tile = wide // GRAD_PARTS
    mine = pl.ds(pl.multiple_of(d * wide, 128), wide)
    theirs = pl.ds(pl.multiple_of((1 - d) * wide, 128), wide)

    def remote(src, dst, ssem, rsem, device):
        return pltpu.make_async_remote_copy(
            src_ref=src, dst_ref=dst, send_sem=ssem, recv_sem=rsem,
            device_id=device, device_id_type=MESH,
        )

    loads = [
        pltpu.make_async_copy(route_in, route, load_sem.at[4]),
        pltpu.make_async_copy(probs_in, probs, load_sem.at[5]),
        pltpu.make_async_copy(tok.at[:, mine], near_tok, load_sem.at[0]),
        pltpu.make_async_copy(w_gate, wg, load_sem.at[1]),
        pltpu.make_async_copy(w_up, wu, load_sem.at[2]),
        pltpu.make_async_copy(w_down, wd, load_sem.at[3]),
    ]
    for load in loads:
        load.start()

    barrier = pltpu.get_barrier_semaphore()
    even = b - c
    greeted = (
        (even, 1 - d),
        (lax.rem(even + 2, n_blk) + 1, d),
        (lax.rem(even + n_blk - 2, n_blk) + 1, d),
    )
    for device in greeted:
        pl.semaphore_signal(barrier, inc=1, device_id=device, device_id_type=MESH)

    @pl.when(c == 0)
    def _():
        pl.semaphore_wait(barrier, 3)
        pl.semaphore_signal(across_in, inc=1, device_id=partner, device_id_type=MESH)

    @pl.when(c == 1)
    def _():
        pl.semaphore_signal(barrier, inc=1, device_id=partner, device_id_type=MESH)
        pl.semaphore_wait(across_in, 1)

    def hear_cycle():
        @pl.when(c == 1)
        def _():
            pl.semaphore_wait(barrier, 4)
            pl.semaphore_signal(cycle_in, inc=1, device_id=partner, device_id_type=MESH)

        @pl.when(c == 0)
        def _():
            pl.semaphore_wait(cycle_in, 1)

    x_tok = remote(tok.at[:, theirs], far_tok, tok_s, tok_r, across)
    x_facts = remote(facts.at[0, 1, c], facts.at[1, 1, c], xf_s, xf_r, across)

    def out_rows(g, k):
        return remote(
            outbox.at[g, k], rows.at[g, 2 * k, c], ob_s.at[g, k], ob_r.at[g, k], (lower, upper)[k]
        )

    def out_facts(g, k):
        return remote(
            facts.at[g, 1, c], facts.at[g, 2 * k, c], of_s.at[g, k], of_r.at[g, k],
            (lower, upper)[k],
        )

    def side_rows(g, j):
        return remote(
            rows.at[g, j, c], rows.at[g, j, c], side_s.at[g, j], side_r.at[g, j], partner
        )

    def side_facts(g, j):
        return remote(facts.at[g, j, c], facts.at[g, j, c], sf_s.at[g, j], sf_r.at[g, j], partner)

    def side_rows_in(g, j):
        return remote(
            rows.at[g, j, other_core], rows.at[g, j, other_core],
            side_s.at[g, j], side_r.at[g, j], partner,
        )

    def side_facts_in(g, j):
        return remote(
            facts.at[g, j, other_core], facts.at[g, j, other_core],
            sf_s.at[g, j], sf_r.at[g, j], partner,
        )

    def x_pre(g, j):
        return remote(
            pre_send.at[g, j], pre_recv.at[1 - g, j], pre_s.at[g, j], pre_r.at[1 - g, j], across
        )

    def o_copy(g, j):
        return remote(o_send.at[g, j], o_recv.at[g, j], o_s.at[g, j], o_r.at[g, j], partner)

    def x_dh(g, j):
        return remote(
            dh_send.at[g, j], dh_recv.at[1 - g, j], dh_s.at[g, j], dh_r.at[1 - g, j], across
        )

    def dx_copy(g, j):
        return remote(
            dx_part.at[g, j, other_core], dx_recv.at[g, j], dx_s.at[g, j], dx_r.at[g, j], partner
        )

    def home_copy(g, k):
        return remote(
            dx_sum.at[g, 2 * k], home.at[g, 2 * k], home_s.at[g, k], home_r.at[g, k],
            (upper, lower)[k],
        )

    x_res = remote(res_far, out_tok.at[:, mine], res_s, res_r, across)

    def choose(g):
        fact = facts[g, 1, c]
        kinds = lax.broadcasted_iota(jnp.int32, fact.shape, 0).astype(F32)
        chosen = jnp.broadcast_to(fact[0:1], fact.shape) == kinds
        place = places_of(chosen.astype(F32))
        kept = jnp.where(chosen, place, -1.0)
        slot = lax.broadcasted_iota(jnp.int32, (CAP, fact.shape[1]), 0).astype(F32)
        for j in range(3):
            key = jnp.broadcast_to(kept[j : j + 1], (CAP, fact.shape[1]))
            sel[g, j] = (slot == key).astype(F32).astype(BF16)

    def pick(g, j, source, target):
        target[...] = dot(sel[g, j], source[...], 1, 0).astype(BF16)

    def front(g, source):
        choose(g)
        pick(g, 0, source, outbox.at[g, 0])
        if g == 0:
            hear_cycle()
        out_rows(g, 0).start()
        pick(g, 2, source, outbox.at[g, 1])
        out_rows(g, 1).start()
        pick(g, 1, source, rows.at[g, 1, c])
        side_rows(g, 1).start()
        for k in range(2):
            out_facts(g, k).start()
        side_facts(g, 1).start()

    x_tok.start()
    pad = jnp.zeros((facts.shape[3] - 2, facts.shape[4]), F32)
    loads[0].wait()
    loads[1].wait()
    facts[0, 1, c] = jnp.concatenate([route[...].astype(F32), probs[...], pad], axis=0)
    x_facts.start()
    loads[2].wait()
    front(0, near_tok)
    loads[3].wait()
    loads[4].wait()

    def forward(g, k):
        out_rows(g, k).wait_recv()
        side_rows(g, 2 * k).start()
        out_facts(g, k).wait_recv()
        side_facts(g, 2 * k).start()

    def first(g, j):
        side_rows_in(g, j).wait_recv()
        unit = rows[g, j].reshape(2 * CAP, wide)
        for part, weight in enumerate((wg, wu)):
            cols = pl.ds(part * hidden, hidden)
            value = dot(unit, weight[...], 1, 0)
            pre[g, j, :, cols] = value
            pre_send[g, j, :, cols] = value.astype(BF16)

    def activate(g, j):
        x_pre(1 - g, j).wait_recv()
        full = pre[g, j] + pre_recv[g, j].astype(F32)
        pre[g, j] = full
        gate, up = full[:, :hidden], full[:, hidden:]
        act = (gate * jax.nn.sigmoid(gate) * up).astype(BF16)
        hid[g, j] = act
        o_send[g, j] = dot(act, wd[...], 1, 1).astype(BF16)
        o_copy(g, j).start()

    def back_unit(g, j):
        side_facts_in(g, j).wait_recv()
        for s in range(2):
            fact = facts[g, j, s]
            chosen = jnp.broadcast_to(fact[0:1], fact.shape) == float(j)
            place = places_of(chosen.astype(F32))
            slots = slots_of(chosen[0:1], place[0:1])
            weight = jnp.where(slots, jnp.broadcast_to(fact[1:2], slots.shape), 0.0)
            gcol[g, j, s] = jnp.broadcast_to(
                jnp.sum(weight, axis=1, keepdims=True), gcol.shape[3:]
            )
        o_copy(g, j).wait_recv()
        gates = gcol[g, j].reshape(2 * CAP, gcol.shape[4])[:, 0:1]
        total = (o_send[g, j].astype(F32) + o_recv[g, j].astype(F32)).astype(BF16)
        rows_back = (gates * (gates * total.astype(F32))).astype(BF16)
        back[g, j] = rows_back
        value = dot(rows_back, wd[...], 1, 0)
        dh[g, j] = value
        dh_send[g, j] = value.astype(BF16)

    def grad_unit(k, left, right, target):
        for n in range(wide // tile):
            cols = pl.ds(n * tile, tile)
            value = dot(
                left[..., cols].reshape(-1, tile), right[...].reshape(-1, hidden), 0, 0
            )
            grads[k, cols, :] = value.astype(BF16)
            pltpu.make_async_copy(
                grads.at[k, cols, :], target.at[cols, :], grad_sem.at[k, n]
            ).start()

    def down_unit(g, j):
        x_dh(1 - g, j).wait_recv()
        d_hidden = dh[g, j] + dh_recv[g, j].astype(F32)
        gate, up = pre[g, j, :, :hidden], pre[g, j, :, hidden:]
        sigmoid = jax.nn.sigmoid(gate)
        d_g = (d_hidden * up * (sigmoid * (1.0 + gate * (1.0 - sigmoid)))).astype(BF16)
        d_u = (d_hidden * (gate * sigmoid)).astype(BF16)
        dgate[g, j] = d_g
        dup[g, j] = d_u
        value = dot(d_g, wg[...], 1, 1) + dot(d_u, wu[...], 1, 1)
        dx_part[g, j] = value.astype(BF16).reshape(2, CAP, wide)
        dx_copy(g, j).start()

    def join_unit(g, j):
        dx_copy(g, j).wait_recv()
        dx_sum[g, j] = (dx_part[g, j, c].astype(F32) + dx_recv[g, j].astype(F32)).astype(BF16)

        if j == 1:
            home[g, j] = dx_sum[g, j]
        else:
            home_copy(g, j // 2).start()

    def unpack(g, target):
        for k in range(2):
            home_copy(g, k).wait_recv()
        tokens = sel.shape[3]
        target[...] = dot(
            sel[g].reshape(3 * CAP, tokens), home[g].reshape(3 * CAP, wide), 0, 0
        ).astype(BF16)

    first(0, 1)
    x_pre(0, 1).start()
    x_facts.wait_recv()
    x_tok.wait_recv()
    front(1, far_tok)
    for k in range(2):
        forward(0, k)
    for j in (0, 2):
        first(0, j)
        x_pre(0, j).start()
    first(1, 1)
    for k in range(2):
        forward(1, k)
    for j in (0, 2):
        first(1, j)
        x_pre(1, j).start()
    loads[5].wait()

    activate(1, 1)
    activate(1, 0)
    back_unit(1, 1)
    activate(1, 2)
    back_unit(1, 0)
    back_unit(1, 2)

    activate(0, 0)
    back_unit(0, 0)
    x_dh(0, 0).start()
    x_pre(1, 1).start()
    activate(0, 2)
    back_unit(0, 2)
    x_dh(0, 2).start()
    x_dh(1, 0).start()
    down_unit(1, 0)
    join_unit(1, 0)
    activate(0, 1)
    back_unit(0, 1)
    x_dh(0, 1).start()
    x_dh(1, 2).start()
    x_dh(1, 1).start()
    down_unit(1, 2)
    join_unit(1, 2)
    down_unit(0, 0)
    down_unit(1, 1)
    join_unit(1, 1)
    unpack(1, res_far)
    x_res.start()
    join_unit(0, 0)
    down_unit(0, 2)
    down_unit(0, 1)
    join_unit(0, 2)
    join_unit(0, 1)
    grad_unit(2, back, hid, out_down)
    grad_unit(0, rows, dgate, out_gate)
    grad_unit(1, rows, dup, out_up)
    unpack(0, res_near)
    near_out = pltpu.make_async_copy(res_near, out_tok.at[:, mine], near_sem)
    near_out.start()

    x_tok.wait_send()
    x_facts.wait_send()
    for g in range(2):
        for k in range(2):
            out_rows(g, k).wait_send()
            out_facts(g, k).wait_send()
            home_copy(g, k).wait_send()
        for j in range(3):
            side_rows(g, j).wait_send()
            side_facts(g, j).wait_send()
            x_pre(g, j).wait_send()
            o_copy(g, j).wait_send()
            x_dh(g, j).wait_send()
            dx_copy(g, j).wait_send()
    for k, target in enumerate((out_gate, out_up, out_down)):
        for n in range(wide // tile):
            cols = pl.ds(n * tile, tile)
            pltpu.make_async_copy(
                grads.at[k, cols, :], target.at[cols, :], grad_sem.at[k, n]
            ).wait()
    near_out.wait()
    x_res.wait_send()
    remote(res_far, out_tok.at[:, theirs], res_s, res_r, across).wait_recv()


def settle_kernel(parts, *refs):
    count = len(refs) // 2
    sources, targets, sem = refs[:count], refs[count : 2 * count], refs[-1]
    copies = []
    for k in range(count):
        rows = sources[k].shape[0] // parts
        for part in range(parts):
            span = pl.ds(part * rows, rows)
            copies.append(
                pltpu.make_async_copy(
                    sources[k].at[span, :], targets[k].at[span, :], sem.at[k, part]
                )
            )
    for copy in copies:
        copy.start()
    for copy in copies:
        copy.wait()


def settled(arrays, parts=4):
    return pl.pallas_call(
        functools.partial(settle_kernel, parts),
        out_shape=tuple(jax.ShapeDtypeStruct(a.shape, a.dtype) for a in arrays),
        in_specs=[pl.BlockSpec(memory_space=pl.ANY)] * len(arrays),
        out_specs=[pl.BlockSpec(memory_space=pltpu.HBM)] * len(arrays),
        scratch_shapes=[pltpu.SemaphoreType.DMA((len(arrays), parts))],
        compiler_params=pltpu.CompilerParams(vmem_limit_bytes=1 << 20),
    )(*arrays)


def in_hbm(array):
    return pltpu.with_memory_space_constraint(array, pltpu.HBM)


def per_device(n_blk, tokens, route_dir, gate_probs, gate_weight, up_weight, down_weight):
    count, model = tokens.shape
    _, wide, hidden = gate_weight.shape
    dma = pltpu.SemaphoreType.DMA
    vmem = pltpu.VMEM
    units = 2 * CAP
    outs = pl.pallas_call(
        functools.partial(kernel, n_blk),
        out_shape=(
            jax.ShapeDtypeStruct((count, model), BF16),
            jax.ShapeDtypeStruct((wide, hidden), BF16),
            jax.ShapeDtypeStruct((wide, hidden), BF16),
            jax.ShapeDtypeStruct((wide, hidden), BF16),
        ),
        in_specs=[
            pl.BlockSpec(memory_space=pltpu.HBM),
            pl.BlockSpec(memory_space=pltpu.HBM),
            pl.BlockSpec(memory_space=pltpu.HBM),
            pl.BlockSpec(memory_space=pltpu.HBM),
            pl.BlockSpec(memory_space=pltpu.HBM),
            pl.BlockSpec(memory_space=pltpu.HBM),
        ],
        out_specs=[pl.BlockSpec(memory_space=pl.ANY)] * 4,
        scratch_shapes=[
            vmem((1, count), jnp.int32),
            vmem((1, count), F32),
            vmem((wide, hidden), BF16),
            vmem((wide, hidden), BF16),
            vmem((wide, hidden), BF16),
            vmem((count, wide), BF16),
            vmem((count, wide), BF16),
            vmem((2, 3, 2, 8, count), F32),
            vmem((2, 3, CAP, count), BF16),
            vmem((2, 2, CAP, wide), BF16),
            vmem((2, 3, 2, CAP, wide), BF16),
            vmem((2, 3, units, 2 * hidden), F32),
            vmem((2, 3, units, 2 * hidden), BF16),
            vmem((2, 3, units, 2 * hidden), BF16),
            vmem((2, 3, units, hidden), BF16),
            vmem((2, 3, units, wide), BF16),
            vmem((2, 3, units, wide), BF16),
            vmem((2, 3, units, wide), BF16),
            vmem((2, 3, 2, CAP, 128), F32),
            vmem((2, 3, units, hidden), F32),
            vmem((2, 3, units, hidden), BF16),
            vmem((2, 3, units, hidden), BF16),
            vmem((2, 3, units, hidden), BF16),
            vmem((2, 3, units, hidden), BF16),
            vmem((2, 3, 2, CAP, wide), BF16),
            vmem((2, 3, CAP, wide), BF16),
            vmem((2, 3, CAP, wide), BF16),
            vmem((2, 3, CAP, wide), BF16),
            vmem((count, wide), BF16),
            vmem((count, wide), BF16),
            vmem((3, wide, hidden), BF16),
            dma((6,)),
            dma, dma, dma, dma,
            dma((2, 2)), dma((2, 2)), dma((2, 2)), dma((2, 2)),
            dma((2, 3)), dma((2, 3)), dma((2, 3)), dma((2, 3)),
            dma((2, 3)), dma((2, 3)), dma((2, 3)), dma((2, 3)),
            dma((2, 3)), dma((2, 3)), dma((2, 3)), dma((2, 3)),
            dma((2, 2)), dma((2, 2)),
            dma, dma,
            dma,
            dma((3, GRAD_PARTS)),
            pltpu.SemaphoreType.REGULAR,
            pltpu.SemaphoreType.REGULAR,
        ],
        compiler_params=pltpu.CompilerParams(
            collective_id=0, has_side_effects=True, vmem_limit_bytes=46 << 20
        ),
    )(
        in_hbm(tokens),
        in_hbm(route_dir.reshape(1, count)),
        in_hbm(gate_probs.reshape(1, count)),
        in_hbm(gate_weight[0]),
        in_hbm(up_weight[0]),
        in_hbm(down_weight[0]),
    )
    d_tokens, grad_gate, grad_up, grad_down = settled(outs)
    return d_tokens, grad_gate[None], grad_up[None], grad_down[None]


def solution(mesh):
    return jax.shard_map(
        functools.partial(per_device, mesh.shape["blk"]),
        mesh=mesh,
        in_specs=(
            P(("blk", "dp"), None),
            P(("blk", "dp"), None),
            P(("blk", "dp"), None),
            P("blk", "dp", None),
            P("blk", "dp", None),
            P("blk", "dp", None),
        ),
        out_specs=(
            P(("blk", "dp"), None),
            P("blk", "dp", None),
            P("blk", "dp", None),
            P("blk", "dp", None),
        ),
        check_vma=False,
    )
```

```python
import functools

import jax
import jax.numpy as jnp
from jax import lax
from jax.experimental import pallas as pl
from jax.experimental.pallas import tpu as pltpu
from jax.sharding import PartitionSpec as P

CAP = 64
GRAD_PARTS = 2
MESH = pl.DeviceIdType.MESH
F32, BF16 = jnp.float32, jnp.bfloat16


def dot(left_side, right_side, left_dim, right_dim):
    return lax.dot_general(
        left_side, right_side, (((left_dim,), (right_dim,)), ((), ())), preferred_element_type=F32
    )


def places_of(chosen):
    tokens = chosen.shape[1]
    before = lax.broadcasted_iota(jnp.int32, (tokens, tokens), 0)
    after = lax.broadcasted_iota(jnp.int32, (tokens, tokens), 1)
    return dot(chosen.astype(BF16), (before <= after).astype(BF16), 1, 0) - 1.0


def slots_of(chosen_row, place_row):
    tokens = chosen_row.shape[1]
    key = jnp.where(chosen_row, place_row, -1.0)
    slot = lax.broadcasted_iota(jnp.int32, (CAP, tokens), 0).astype(F32)
    return slot == jnp.broadcast_to(key, (CAP, tokens))


def kernel(
    n_blk,
    tok, route_in, probs_in, w_gate, w_up, w_down,
    out_tok, out_gate, out_up, out_down,
    route, probs, wg, wu, wd, wg_t, wu_t, near_tok, far_tok, facts, sel, outbox, rows,
    pre, pre_send, pre_recv, hid, o_send, o_recv, back, gcol,
    dh, dh_send, dh_recv, dgu, dx_part, dx_recv, home,
    res_far, grads,
    load_sem, tok_s, tok_r, xf_s, xf_r, ob_s, ob_r, of_s, of_r, side_s, side_r, sf_s, sf_r,
    pre_s, pre_r, o_s, o_r, dh_s, dh_r, dx_s, dx_r, home_s, home_r, res_s, res_r,
    near_sem, grad_sem, across_in, cycle_in,
):
    b, d = lax.axis_index("blk"), lax.axis_index("dp")
    c = lax.rem(b, 2)
    other_core = 1 - c
    partner, across = (b + 1 - 2 * c, d), (b, 1 - d)
    upper, lower = (lax.rem(b + 2, n_blk), d), (lax.rem(b + n_blk - 2, n_blk), d)
    wide = near_tok.shape[1]
    hidden = wg.shape[1]
    tile = wide // GRAD_PARTS
    mine = pl.ds(pl.multiple_of(d * wide, 128), wide)
    theirs = pl.ds(pl.multiple_of((1 - d) * wide, 128), wide)

    def remote(src, dst, ssem, rsem, device):
        return pltpu.make_async_remote_copy(
            src_ref=src, dst_ref=dst, send_sem=ssem, recv_sem=rsem,
            device_id=device, device_id_type=MESH,
        )

    loads = [
        pltpu.make_async_copy(route_in, route, load_sem.at[4]),
        pltpu.make_async_copy(probs_in, probs, load_sem.at[5]),
        pltpu.make_async_copy(tok.at[:, mine], near_tok, load_sem.at[0]),
        pltpu.make_async_copy(w_gate, wg, load_sem.at[1]),
        pltpu.make_async_copy(w_up, wu, load_sem.at[2]),
        pltpu.make_async_copy(w_down, wd, load_sem.at[3]),
    ]
    for load in loads:
        load.start()

    barrier = pltpu.get_barrier_semaphore()
    even = b - c
    greeted = (
        (even, 1 - d),
        (lax.rem(even + 2, n_blk) + 1, d),
        (lax.rem(even + n_blk - 2, n_blk) + 1, d),
    )
    for device in greeted:
        pl.semaphore_signal(barrier, inc=1, device_id=device, device_id_type=MESH)

    @pl.when(c == 0)
    def _():
        pl.semaphore_wait(barrier, 3)
        pl.semaphore_signal(across_in, inc=1, device_id=partner, device_id_type=MESH)

    @pl.when(c == 1)
    def _():
        pl.semaphore_signal(barrier, inc=1, device_id=partner, device_id_type=MESH)
        pl.semaphore_wait(across_in, 1)

    def hear_cycle():
        @pl.when(c == 1)
        def _():
            pl.semaphore_wait(barrier, 4)
            pl.semaphore_signal(cycle_in, inc=1, device_id=partner, device_id_type=MESH)

        @pl.when(c == 0)
        def _():
            pl.semaphore_wait(cycle_in, 1)

    x_tok = remote(tok.at[:, theirs], far_tok, tok_s, tok_r, across)
    x_facts = remote(facts.at[0, 1, c], facts.at[1, 1, c], xf_s, xf_r, across)

    def out_rows(g, k):
        return remote(
            outbox.at[g, k], rows.at[g, 2 * k, c], ob_s.at[g, k], ob_r.at[g, k], (lower, upper)[k]
        )

    def out_facts(g, k):
        return remote(
            facts.at[g, 1, c], facts.at[g, 2 * k, c], of_s.at[g, k], of_r.at[g, k],
            (lower, upper)[k],
        )

    def side_rows(g, j):
        return remote(
            rows.at[g, j, c], rows.at[g, j, c], side_s.at[g, j], side_r.at[g, j], partner
        )

    def side_facts(g, j):
        return remote(facts.at[g, j, c], facts.at[g, j, c], sf_s.at[g, j], sf_r.at[g, j], partner)

    def side_rows_in(g, j):
        return remote(
            rows.at[g, j, other_core], rows.at[g, j, other_core],
            side_s.at[g, j], side_r.at[g, j], partner,
        )

    def side_facts_in(g, j):
        return remote(
            facts.at[g, j, other_core], facts.at[g, j, other_core],
            sf_s.at[g, j], sf_r.at[g, j], partner,
        )

    def x_pre(g, j):
        return remote(
            pre_send.at[g, j], pre_recv.at[1 - g, j], pre_s.at[g, j], pre_r.at[1 - g, j], across
        )

    def o_copy(g, j):
        return remote(o_send.at[g, j], o_recv.at[g, j], o_s.at[g, j], o_r.at[g, j], partner)

    def x_dh(g, j):
        return remote(
            dh_send.at[g, j], dh_recv.at[1 - g, j], dh_s.at[g, j], dh_r.at[1 - g, j], across
        )

    def dx_copy(g, j):
        return remote(
            dx_part.at[g, j, other_core], dx_recv.at[g, j], dx_s.at[g, j], dx_r.at[g, j], partner
        )

    def home_copy(g, k):
        return remote(
            dx_part.at[g, 2 * k, c], home.at[g, 2 * k], home_s.at[g, k], home_r.at[g, k],
            (upper, lower)[k],
        )

    x_res = remote(res_far, out_tok.at[:, mine], res_s, res_r, across)

    def choose(g):
        fact = facts[g, 1, c]
        kinds = lax.broadcasted_iota(jnp.int32, fact.shape, 0).astype(F32)
        chosen = jnp.broadcast_to(fact[0:1], fact.shape) == kinds
        place = places_of(chosen.astype(F32))
        kept = jnp.where(chosen, place, -1.0)
        slot = lax.broadcasted_iota(jnp.int32, (CAP, fact.shape[1]), 0).astype(F32)
        for j in range(3):
            key = jnp.broadcast_to(kept[j : j + 1], (CAP, fact.shape[1]))
            sel[g, j] = (slot == key).astype(F32).astype(BF16)

    def pick(g, j, source, target):
        target[...] = dot(sel[g, j], source[...], 1, 0).astype(BF16)

    def front(g, source):
        choose(g)
        pick(g, 0, source, outbox.at[g, 0])
        if g == 0:
            hear_cycle()
        out_rows(g, 0).start()
        pick(g, 2, source, outbox.at[g, 1])
        out_rows(g, 1).start()
        pick(g, 1, source, rows.at[g, 1, c])
        side_rows(g, 1).start()
        for k in range(2):
            out_facts(g, k).start()
        side_facts(g, 1).start()

    x_tok.start()
    pad = jnp.zeros((facts.shape[3] - 2, facts.shape[4]), F32)
    loads[0].wait()
    loads[1].wait()
    facts[0, 1, c] = jnp.concatenate([route[...].astype(F32), probs[...], pad], axis=0)
    x_facts.start()
    loads[2].wait()
    front(0, near_tok)
    loads[3].wait()
    loads[4].wait()

    def forward(g, k):
        out_rows(g, k).wait_recv()
        side_rows(g, 2 * k).start()
        out_facts(g, k).wait_recv()
        side_facts(g, 2 * k).start()

    def first(g, j):
        side_rows_in(g, j).wait_recv()
        unit = rows[g, j].reshape(2 * CAP, wide)
        for part, weight in enumerate((wg, wu)):
            cols = pl.ds(part * hidden, hidden)
            value = dot(unit, weight[...], 1, 0)
            pre[g, j, :, cols] = value
            pre_send[g, j, :, cols] = value.astype(BF16)

    def activate(g, j):
        x_pre(1 - g, j).wait_recv()
        full = pre[g, j] + pre_recv[g, j].astype(F32)
        pre[g, j] = full
        gate, up = full[:, :hidden], full[:, hidden:]
        act = (gate * jax.nn.sigmoid(gate) * up).astype(BF16)
        hid[g, j] = act
        o_send[g, j] = dot(act, wd[...], 1, 1).astype(BF16)
        o_copy(g, j).start()

    def back_unit(g, j):
        side_facts_in(g, j).wait_recv()
        for s in range(2):
            fact = facts[g, j, s]
            chosen = jnp.broadcast_to(fact[0:1], fact.shape) == float(j)
            place = places_of(chosen.astype(F32))
            slots = slots_of(chosen[0:1], place[0:1])
            weight = jnp.where(slots, jnp.broadcast_to(fact[1:2], slots.shape), 0.0)
            gcol[g, j, s] = jnp.broadcast_to(
                jnp.sum(weight, axis=1, keepdims=True), gcol.shape[3:]
            )
        o_copy(g, j).wait_recv()
        gates = gcol[g, j].reshape(2 * CAP, gcol.shape[4])[:, 0:1]
        total = (o_send[g, j].astype(F32) + o_recv[g, j].astype(F32)).astype(BF16)
        rows_back = (gates * (gates * total.astype(F32))).astype(BF16)
        back[g, j] = rows_back
        value = dot(rows_back, wd[...], 1, 0)
        dh[g, j] = value
        dh_send[g, j] = value.astype(BF16)

    def grad_unit(left, right, targets):
        for n in range(wide // tile):
            cols = pl.ds(n * tile, tile)
            value = dot(
                left[..., cols].reshape(-1, tile), right[...].reshape(-1, right.shape[3]), 0, 0
            )
            for part, (k, target) in enumerate(targets):
                own = value[:, part * hidden : (part + 1) * hidden]
                grads[k, cols, :] = own.astype(BF16)
                pltpu.make_async_copy(
                    grads.at[k, cols, :], target.at[cols, :], grad_sem.at[k, n]
                ).start()

    def down_unit(g, j):
        x_dh(1 - g, j).wait_recv()
        d_hidden = dh[g, j] + dh_recv[g, j].astype(F32)
        gate, up = pre[g, j, :, :hidden], pre[g, j, :, hidden:]
        sigmoid = jax.nn.sigmoid(gate)
        d_g = (d_hidden * up * (sigmoid * (1.0 + gate * (1.0 - sigmoid)))).astype(BF16)
        d_u = (d_hidden * (gate * sigmoid)).astype(BF16)
        dgu[g, j, :, :hidden] = d_g
        dgu[g, j, :, hidden:] = d_u
        value = dot(d_g, wg_t[...], 1, 0) + dot(d_u, wu_t[...], 1, 0)
        dx_part[g, j] = value.astype(BF16).reshape(2, CAP, wide)
        dx_copy(g, j).start()

    def join_unit(g, j, leave=True):
        dx_copy(g, j).wait_recv()
        total = (dx_part[g, j, c].astype(F32) + dx_recv[g, j].astype(F32)).astype(BF16)

        if j == 1:
            home[g, j] = total
        else:
            dx_part[g, j, c] = total
            if leave:
                home_copy(g, j // 2).start()

    def arrive(g):
        for k in range(2):
            home_copy(g, k).wait_recv()

    def unpack(g, target):
        tokens = sel.shape[3]
        target[...] = dot(
            sel[g].reshape(3 * CAP, tokens), home[g].reshape(3 * CAP, wide), 0, 0
        ).astype(BF16)

    first(0, 1)
    x_pre(0, 1).start()
    for plain, turned in ((wg, wg_t), (wu, wu_t)):
        turned[...] = plain[...].T
    x_facts.wait_recv()
    x_tok.wait_recv()
    front(1, far_tok)
    for k in range(2):
        forward(0, k)
    for j in (0, 2):
        first(0, j)
        x_pre(0, j).start()
    first(1, 1)
    for k in range(2):
        forward(1, k)
    for j in (0, 2):
        first(1, j)
        x_pre(1, j).start()
    loads[5].wait()

    activate(1, 1)
    activate(1, 0)
    back_unit(1, 1)
    activate(1, 2)
    back_unit(1, 0)
    back_unit(1, 2)

    activate(0, 0)
    back_unit(0, 0)
    x_dh(0, 0).start()
    x_pre(1, 1).start()
    activate(0, 2)
    back_unit(0, 2)
    x_dh(0, 2).start()
    x_dh(1, 0).start()
    down_unit(1, 0)
    join_unit(1, 0)
    activate(0, 1)
    back_unit(0, 1)
    x_dh(0, 1).start()
    x_dh(1, 2).start()
    x_dh(1, 1).start()
    down_unit(1, 2)
    join_unit(1, 2)
    down_unit(0, 0)
    down_unit(1, 1)
    join_unit(1, 1)
    join_unit(0, 0, leave=False)
    arrive(1)
    home_copy(0, 0).start()
    unpack(1, res_far)
    x_res.start()
    down_unit(0, 2)
    join_unit(0, 2)
    down_unit(0, 1)
    join_unit(0, 1)
    grad_unit(back, hid, ((2, out_down),))
    grad_unit(rows, dgu, ((0, out_gate), (1, out_up)))
    arrive(0)
    unpack(0, near_tok)
    near_out = pltpu.make_async_copy(near_tok, out_tok.at[:, mine], near_sem)
    near_out.start()

    x_tok.wait_send()
    x_facts.wait_send()
    for g in range(2):
        for k in range(2):
            out_rows(g, k).wait_send()
            out_facts(g, k).wait_send()
            home_copy(g, k).wait_send()
        for j in range(3):
            side_rows(g, j).wait_send()
            side_facts(g, j).wait_send()
            x_pre(g, j).wait_send()
            o_copy(g, j).wait_send()
            x_dh(g, j).wait_send()
            dx_copy(g, j).wait_send()
    for k, target in enumerate((out_gate, out_up, out_down)):
        for n in range(wide // tile):
            cols = pl.ds(n * tile, tile)
            pltpu.make_async_copy(
                grads.at[k, cols, :], target.at[cols, :], grad_sem.at[k, n]
            ).wait()
    near_out.wait()
    x_res.wait_send()
    remote(res_far, out_tok.at[:, theirs], res_s, res_r, across).wait_recv()


def settle_kernel(parts, *refs):
    count = len(refs) // 2
    sources, targets, sem = refs[:count], refs[count : 2 * count], refs[-1]
    copies = []
    for k in range(count):
        rows = sources[k].shape[0] // parts
        for part in range(parts):
            span = pl.ds(part * rows, rows)
            copies.append(
                pltpu.make_async_copy(
                    sources[k].at[span, :], targets[k].at[span, :], sem.at[k, part]
                )
            )
    for copy in copies:
        copy.start()
    for copy in copies:
        copy.wait()


def settled(arrays, parts=2):
    return pl.pallas_call(
        functools.partial(settle_kernel, parts),
        out_shape=tuple(jax.ShapeDtypeStruct(a.shape, a.dtype) for a in arrays),
        in_specs=[pl.BlockSpec(memory_space=pl.ANY)] * len(arrays),
        out_specs=[pl.BlockSpec(memory_space=pltpu.HBM)] * len(arrays),
        scratch_shapes=[pltpu.SemaphoreType.DMA((len(arrays), parts))],
        compiler_params=pltpu.CompilerParams(vmem_limit_bytes=1 << 20),
    )(*arrays)


def in_hbm(array):
    return pltpu.with_memory_space_constraint(array, pltpu.HBM)


def per_device(n_blk, tokens, route_dir, gate_probs, gate_weight, up_weight, down_weight):
    count, model = tokens.shape
    _, wide, hidden = gate_weight.shape
    dma = pltpu.SemaphoreType.DMA
    vmem = pltpu.VMEM
    units = 2 * CAP
    outs = pl.pallas_call(
        functools.partial(kernel, n_blk),
        out_shape=(
            jax.ShapeDtypeStruct((count, model), BF16),
            jax.ShapeDtypeStruct((wide, hidden), BF16),
            jax.ShapeDtypeStruct((wide, hidden), BF16),
            jax.ShapeDtypeStruct((wide, hidden), BF16),
        ),
        in_specs=[
            pl.BlockSpec(memory_space=pltpu.HBM),
            pl.BlockSpec(memory_space=pltpu.HBM),
            pl.BlockSpec(memory_space=pltpu.HBM),
            pl.BlockSpec(memory_space=pltpu.HBM),
            pl.BlockSpec(memory_space=pltpu.HBM),
            pl.BlockSpec(memory_space=pltpu.HBM),
        ],
        out_specs=[pl.BlockSpec(memory_space=pl.ANY)] * 4,
        scratch_shapes=[
            vmem((1, count), jnp.int32),
            vmem((1, count), F32),
            vmem((wide, hidden), BF16),
            vmem((wide, hidden), BF16),
            vmem((wide, hidden), BF16),
            vmem((hidden, wide), BF16),
            vmem((hidden, wide), BF16),
            vmem((count, wide), BF16),
            vmem((count, wide), BF16),
            vmem((2, 3, 2, 8, count), F32),
            vmem((2, 3, CAP, count), BF16),
            vmem((2, 2, CAP, wide), BF16),
            vmem((2, 3, 2, CAP, wide), BF16),
            vmem((2, 3, units, 2 * hidden), F32),
            vmem((2, 3, units, 2 * hidden), BF16),
            vmem((2, 3, units, 2 * hidden), BF16),
            vmem((2, 3, units, hidden), BF16),
            vmem((2, 3, units, wide), BF16),
            vmem((2, 3, units, wide), BF16),
            vmem((2, 3, units, wide), BF16),
            vmem((2, 3, 2, CAP, 128), F32),
            vmem((2, 3, units, hidden), F32),
            vmem((2, 3, units, hidden), BF16),
            vmem((2, 3, units, hidden), BF16),
            vmem((2, 3, units, 2 * hidden), BF16),
            vmem((2, 3, 2, CAP, wide), BF16),
            vmem((2, 3, CAP, wide), BF16),
            vmem((2, 3, CAP, wide), BF16),
            vmem((count, wide), BF16),
            vmem((3, wide, hidden), BF16),
            dma((6,)),
            dma, dma, dma, dma,
            dma((2, 2)), dma((2, 2)), dma((2, 2)), dma((2, 2)),
            dma((2, 3)), dma((2, 3)), dma((2, 3)), dma((2, 3)),
            dma((2, 3)), dma((2, 3)), dma((2, 3)), dma((2, 3)),
            dma((2, 3)), dma((2, 3)), dma((2, 3)), dma((2, 3)),
            dma((2, 2)), dma((2, 2)),
            dma, dma,
            dma,
            dma((3, GRAD_PARTS)),
            pltpu.SemaphoreType.REGULAR,
            pltpu.SemaphoreType.REGULAR,
        ],
        compiler_params=pltpu.CompilerParams(
            collective_id=0, has_side_effects=True, vmem_limit_bytes=46 << 20
        ),
    )(
        in_hbm(tokens),
        in_hbm(route_dir.reshape(1, count)),
        in_hbm(gate_probs.reshape(1, count)),
        in_hbm(gate_weight[0]),
        in_hbm(up_weight[0]),
        in_hbm(down_weight[0]),
    )
    d_tokens, grad_gate, grad_up, grad_down = settled(outs)
    return d_tokens, grad_gate[None], grad_up[None], grad_down[None]


def solution(mesh):
    return jax.shard_map(
        functools.partial(per_device, mesh.shape["blk"]),
        mesh=mesh,
        in_specs=(
            P(("blk", "dp"), None),
            P(("blk", "dp"), None),
            P(("blk", "dp"), None),
            P("blk", "dp", None),
            P("blk", "dp", None),
            P("blk", "dp", None),
        ),
        out_specs=(
            P(("blk", "dp"), None),
            P("blk", "dp", None),
            P("blk", "dp", None),
            P("blk", "dp", None),
        ),
        check_vma=False,
    )
```

```python
import functools

import jax
import jax.numpy as jnp
from jax import lax
from jax.experimental import pallas as pl
from jax.experimental.pallas import tpu as pltpu
from jax.sharding import PartitionSpec as P

CAP = 64
GRAD_PARTS = 2
MESH = pl.DeviceIdType.MESH
F32, BF16 = jnp.float32, jnp.bfloat16


def dot(left_side, right_side, left_dim, right_dim):
    return lax.dot_general(
        left_side, right_side, (((left_dim,), (right_dim,)), ((), ())), preferred_element_type=F32
    )


def places_of(chosen):
    tokens = chosen.shape[1]
    before = lax.broadcasted_iota(jnp.int32, (tokens, tokens), 0)
    after = lax.broadcasted_iota(jnp.int32, (tokens, tokens), 1)
    return dot(chosen.astype(BF16), (before <= after).astype(BF16), 1, 0) - 1.0


def slots_of(chosen_row, place_row):
    tokens = chosen_row.shape[1]
    key = jnp.where(chosen_row, place_row, -1.0)
    slot = lax.broadcasted_iota(jnp.int32, (CAP, tokens), 0).astype(F32)
    return slot == jnp.broadcast_to(key, (CAP, tokens))


def kernel(
    n_blk,
    tok, route_in, probs_in, w_gate, w_up, w_down,
    out_tok, out_gate, out_up, out_down,
    route, probs, wg, wu, wd, wg_t, wu_t, near_tok, far_tok, facts, sel, outbox, rows,
    pre, pre_send, pre_recv, hid, o_send, o_recv, back, gcol,
    dh, dh_send, dh_recv, dgu, dx_part, dx_recv, home,
    res_far, grads,
    load_sem, tok_s, tok_r, xf_s, xf_r, ob_s, ob_r, of_s, of_r, side_s, side_r, sf_s, sf_r,
    pre_s, pre_r, o_s, o_r, dh_s, dh_r, dx_s, dx_r, home_s, home_r, res_s, res_r,
    near_sem, grad_sem, across_in, cycle_in,
):
    b, d = lax.axis_index("blk"), lax.axis_index("dp")
    c = lax.rem(b, 2)
    other_core = 1 - c
    partner, across = (b + 1 - 2 * c, d), (b, 1 - d)
    upper, lower = (lax.rem(b + 2, n_blk), d), (lax.rem(b + n_blk - 2, n_blk), d)
    wide = near_tok.shape[1]
    hidden = wg.shape[1]
    tile = wide // GRAD_PARTS
    mine = pl.ds(pl.multiple_of(d * wide, 128), wide)
    theirs = pl.ds(pl.multiple_of((1 - d) * wide, 128), wide)

    def remote(src, dst, ssem, rsem, device):
        return pltpu.make_async_remote_copy(
            src_ref=src, dst_ref=dst, send_sem=ssem, recv_sem=rsem,
            device_id=device, device_id_type=MESH,
        )

    loads = [
        pltpu.make_async_copy(route_in, route, load_sem.at[4]),
        pltpu.make_async_copy(probs_in, probs, load_sem.at[5]),
        pltpu.make_async_copy(tok.at[:, mine], near_tok, load_sem.at[0]),
        pltpu.make_async_copy(w_gate, wg, load_sem.at[1]),
        pltpu.make_async_copy(w_up, wu, load_sem.at[2]),
        pltpu.make_async_copy(w_down, wd, load_sem.at[3]),
    ]
    for load in loads:
        load.start()

    barrier = pltpu.get_barrier_semaphore()
    even = b - c
    greeted = (
        (even, 1 - d),
        (lax.rem(even + 2, n_blk) + 1, d),
        (lax.rem(even + n_blk - 2, n_blk) + 1, d),
    )
    for device in greeted:
        pl.semaphore_signal(barrier, inc=1, device_id=device, device_id_type=MESH)

    @pl.when(c == 0)
    def _():
        pl.semaphore_wait(barrier, 3)
        pl.semaphore_signal(across_in, inc=1, device_id=partner, device_id_type=MESH)

    @pl.when(c == 1)
    def _():
        pl.semaphore_signal(barrier, inc=1, device_id=partner, device_id_type=MESH)
        pl.semaphore_wait(across_in, 1)

    def hear_cycle():
        @pl.when(c == 1)
        def _():
            pl.semaphore_wait(barrier, 4)
            pl.semaphore_signal(cycle_in, inc=1, device_id=partner, device_id_type=MESH)

        @pl.when(c == 0)
        def _():
            pl.semaphore_wait(cycle_in, 1)

    x_tok = remote(tok.at[:, theirs], far_tok, tok_s, tok_r, across)
    x_facts = remote(facts.at[0, 1, c], facts.at[1, 1, c], xf_s, xf_r, across)

    def out_rows(g, k):
        return remote(
            outbox.at[g, k], rows.at[g, 2 * k, c], ob_s.at[g, k], ob_r.at[g, k], (lower, upper)[k]
        )

    def out_facts(g, k):
        return remote(
            facts.at[g, 1, c], facts.at[g, 2 * k, c], of_s.at[g, k], of_r.at[g, k],
            (lower, upper)[k],
        )

    def side_rows(g, j):
        return remote(
            rows.at[g, j, c], rows.at[g, j, c], side_s.at[g, j], side_r.at[g, j], partner
        )

    def side_facts(g, j):
        return remote(facts.at[g, j, c], facts.at[g, j, c], sf_s.at[g, j], sf_r.at[g, j], partner)

    def side_rows_in(g, j):
        return remote(
            rows.at[g, j, other_core], rows.at[g, j, other_core],
            side_s.at[g, j], side_r.at[g, j], partner,
        )

    def side_facts_in(g, j):
        return remote(
            facts.at[g, j, other_core], facts.at[g, j, other_core],
            sf_s.at[g, j], sf_r.at[g, j], partner,
        )

    def x_pre(g, j):
        return remote(
            pre_send.at[g, j], pre_recv.at[1 - g, j], pre_s.at[g, j], pre_r.at[1 - g, j], across
        )

    def o_copy(g, j):
        return remote(o_send.at[g, j], o_recv.at[g, j], o_s.at[g, j], o_r.at[g, j], partner)

    def x_dh(g, j):
        return remote(
            dh_send.at[g, j], dh_recv.at[1 - g, j], dh_s.at[g, j], dh_r.at[1 - g, j], across
        )

    def dx_copy(g, j):
        return remote(
            dx_part.at[g, j, other_core], dx_recv.at[g, j], dx_s.at[g, j], dx_r.at[g, j], partner
        )

    def home_copy(g, k):
        return remote(
            dx_part.at[g, 2 * k, c], home.at[g, 2 * k], home_s.at[g, k], home_r.at[g, k],
            (upper, lower)[k],
        )

    x_res = remote(res_far, out_tok.at[:, mine], res_s, res_r, across)

    def choose(g):
        fact = facts[g, 1, c]
        kinds = lax.broadcasted_iota(jnp.int32, fact.shape, 0).astype(F32)
        chosen = jnp.broadcast_to(fact[0:1], fact.shape) == kinds
        place = places_of(chosen.astype(F32))
        kept = jnp.where(chosen, place, -1.0)
        slot = lax.broadcasted_iota(jnp.int32, (CAP, fact.shape[1]), 0).astype(F32)
        for j in range(3):
            key = jnp.broadcast_to(kept[j : j + 1], (CAP, fact.shape[1]))
            sel[g, j] = (slot == key).astype(F32).astype(BF16)

    def pick(g, j, source, target):
        target[...] = dot(sel[g, j], source[...], 1, 0).astype(BF16)

    def front(g, source):
        choose(g)
        pick(g, 0, source, outbox.at[g, 0])
        if g == 0:
            hear_cycle()
        out_rows(g, 0).start()
        pick(g, 2, source, outbox.at[g, 1])
        out_rows(g, 1).start()
        pick(g, 1, source, rows.at[g, 1, c])
        side_rows(g, 1).start()
        for k in range(2):
            out_facts(g, k).start()
        side_facts(g, 1).start()

    x_tok.start()
    pad = jnp.zeros((facts.shape[3] - 2, facts.shape[4]), F32)
    loads[0].wait()
    loads[1].wait()
    facts[0, 1, c] = jnp.concatenate([route[...].astype(F32), probs[...], pad], axis=0)
    x_facts.start()
    loads[2].wait()
    front(0, near_tok)
    loads[3].wait()
    loads[4].wait()

    def forward(g, k):
        out_rows(g, k).wait_recv()
        side_rows(g, 2 * k).start()
        out_facts(g, k).wait_recv()
        side_facts(g, 2 * k).start()

    def first(g, j):
        side_rows_in(g, j).wait_recv()
        unit = rows[g, j].reshape(2 * CAP, wide)
        for part, weight in enumerate((wg, wu)):
            cols = pl.ds(part * hidden, hidden)
            value = dot(unit, weight[...], 1, 0)
            pre[g, j, :, cols] = value
            pre_send[g, j, :, cols] = value.astype(BF16)

    def activate(g, j):
        x_pre(1 - g, j).wait_recv()
        full = pre[g, j] + pre_recv[g, j].astype(F32)
        pre[g, j] = full
        gate, up = full[:, :hidden], full[:, hidden:]
        act = (gate * jax.nn.sigmoid(gate) * up).astype(BF16)
        hid[g, j] = act
        o_send[g, j] = dot(act, wd[...], 1, 1).astype(BF16)
        o_copy(g, j).start()

    def back_unit(g, j):
        side_facts_in(g, j).wait_recv()
        for s in range(2):
            fact = facts[g, j, s]
            chosen = jnp.broadcast_to(fact[0:1], fact.shape) == float(j)
            place = places_of(chosen.astype(F32))
            slots = slots_of(chosen[0:1], place[0:1])
            weight = jnp.where(slots, jnp.broadcast_to(fact[1:2], slots.shape), 0.0)
            gcol[g, j, s] = jnp.broadcast_to(
                jnp.sum(weight, axis=1, keepdims=True), gcol.shape[3:]
            )
        o_copy(g, j).wait_recv()
        gates = gcol[g, j].reshape(2 * CAP, gcol.shape[4])[:, 0:1]
        total = (o_send[g, j].astype(F32) + o_recv[g, j].astype(F32)).astype(BF16)
        rows_back = (gates * (gates * total.astype(F32))).astype(BF16)
        back[g, j] = rows_back
        value = dot(rows_back, wd[...], 1, 0)
        dh[g, j] = value
        dh_send[g, j] = value.astype(BF16)

    def grad_unit(left, right, targets):
        for n in range(wide // tile):
            cols = pl.ds(n * tile, tile)
            value = dot(
                left[..., cols].reshape(-1, tile), right[...].reshape(-1, right.shape[3]), 0, 0
            )
            for part, (k, target) in enumerate(targets):
                own = value[:, part * hidden : (part + 1) * hidden]
                grads[k, cols, :] = own.astype(BF16)
                pltpu.make_async_copy(
                    grads.at[k, cols, :], target.at[cols, :], grad_sem.at[k, n]
                ).start()

    def down_unit(g, j):
        x_dh(1 - g, j).wait_recv()
        d_hidden = dh[g, j] + dh_recv[g, j].astype(F32)
        gate, up = pre[g, j, :, :hidden], pre[g, j, :, hidden:]
        sigmoid = jax.nn.sigmoid(gate)
        d_g = (d_hidden * up * (sigmoid * (1.0 + gate * (1.0 - sigmoid)))).astype(BF16)
        d_u = (d_hidden * (gate * sigmoid)).astype(BF16)
        dgu[g, j, :, :hidden] = d_g
        dgu[g, j, :, hidden:] = d_u
        value = dot(d_g, wg_t[...], 1, 0) + dot(d_u, wu_t[...], 1, 0)
        dx_part[g, j] = value.astype(BF16).reshape(2, CAP, wide)
        dx_copy(g, j).start()

    def join_unit(g, j, leave=True):
        dx_copy(g, j).wait_recv()
        total = (dx_part[g, j, c].astype(F32) + dx_recv[g, j].astype(F32)).astype(BF16)

        if j == 1:
            home[g, j] = total
        else:
            dx_part[g, j, c] = total
            if leave:
                home_copy(g, j // 2).start()

    def arrive(g):
        for k in range(2):
            home_copy(g, k).wait_recv()

    def unpack(g, target):
        tokens = sel.shape[3]
        target[...] = dot(
            sel[g].reshape(3 * CAP, tokens), home[g].reshape(3 * CAP, wide), 0, 0
        ).astype(BF16)

    first(0, 1)
    x_pre(0, 1).start()
    for plain, turned in ((wg, wg_t), (wu, wu_t)):
        turned[...] = plain[...].T
    x_facts.wait_recv()
    x_tok.wait_recv()
    front(1, far_tok)
    for k in range(2):
        forward(0, k)
    for j in (0, 2):
        first(0, j)
        x_pre(0, j).start()
    first(1, 1)
    for k in range(2):
        forward(1, k)
    for j in (0, 2):
        first(1, j)
        x_pre(1, j).start()
    loads[5].wait()

    activate(1, 1)
    activate(1, 0)
    back_unit(1, 1)
    activate(1, 2)
    back_unit(1, 0)
    back_unit(1, 2)

    activate(0, 0)
    back_unit(0, 0)
    x_dh(0, 0).start()
    x_pre(1, 1).start()
    activate(0, 2)
    back_unit(0, 2)
    x_dh(0, 2).start()
    x_dh(1, 2).start()
    down_unit(1, 0)
    join_unit(1, 0)
    activate(0, 1)
    back_unit(0, 1)
    x_dh(0, 1).start()
    x_dh(1, 0).start()
    x_dh(1, 1).start()
    down_unit(1, 2)
    join_unit(1, 2)
    down_unit(0, 2)
    down_unit(1, 1)
    join_unit(1, 1)
    join_unit(0, 2, leave=False)
    arrive(1)
    home_copy(0, 1).start()
    unpack(1, res_far)
    x_res.start()
    down_unit(0, 0)
    join_unit(0, 0)
    down_unit(0, 1)
    join_unit(0, 1)
    grad_unit(back, hid, ((2, out_down),))
    grad_unit(rows, dgu, ((0, out_gate), (1, out_up)))
    arrive(0)
    unpack(0, near_tok)
    near_out = pltpu.make_async_copy(near_tok, out_tok.at[:, mine], near_sem)
    near_out.start()

    x_tok.wait_send()
    x_facts.wait_send()
    for g in range(2):
        for k in range(2):
            out_rows(g, k).wait_send()
            out_facts(g, k).wait_send()
            home_copy(g, k).wait_send()
        for j in range(3):
            side_rows(g, j).wait_send()
            side_facts(g, j).wait_send()
            x_pre(g, j).wait_send()
            o_copy(g, j).wait_send()
            x_dh(g, j).wait_send()
            dx_copy(g, j).wait_send()
    for k, target in enumerate((out_gate, out_up, out_down)):
        for n in range(wide // tile):
            cols = pl.ds(n * tile, tile)
            pltpu.make_async_copy(
                grads.at[k, cols, :], target.at[cols, :], grad_sem.at[k, n]
            ).wait()
    near_out.wait()
    x_res.wait_send()
    remote(res_far, out_tok.at[:, theirs], res_s, res_r, across).wait_recv()


def settle_kernel(parts, *refs):
    count = len(refs) // 2
    sources, targets, sem = refs[:count], refs[count : 2 * count], refs[-1]
    copies = []
    for k in range(count):
        rows = sources[k].shape[0] // parts
        for part in range(parts):
            span = pl.ds(part * rows, rows)
            copies.append(
                pltpu.make_async_copy(
                    sources[k].at[span, :], targets[k].at[span, :], sem.at[k, part]
                )
            )
    for copy in copies:
        copy.start()
    for copy in copies:
        copy.wait()


def settled(arrays, parts=2):
    return pl.pallas_call(
        functools.partial(settle_kernel, parts),
        out_shape=tuple(jax.ShapeDtypeStruct(a.shape, a.dtype) for a in arrays),
        in_specs=[pl.BlockSpec(memory_space=pl.ANY)] * len(arrays),
        out_specs=[pl.BlockSpec(memory_space=pltpu.HBM)] * len(arrays),
        scratch_shapes=[pltpu.SemaphoreType.DMA((len(arrays), parts))],
        compiler_params=pltpu.CompilerParams(vmem_limit_bytes=1 << 20),
    )(*arrays)


def in_hbm(array):
    return pltpu.with_memory_space_constraint(array, pltpu.HBM)


def per_device(n_blk, tokens, route_dir, gate_probs, gate_weight, up_weight, down_weight):
    count, model = tokens.shape
    _, wide, hidden = gate_weight.shape
    dma = pltpu.SemaphoreType.DMA
    vmem = pltpu.VMEM
    units = 2 * CAP
    outs = pl.pallas_call(
        functools.partial(kernel, n_blk),
        out_shape=(
            jax.ShapeDtypeStruct((count, model), BF16),
            jax.ShapeDtypeStruct((wide, hidden), BF16),
            jax.ShapeDtypeStruct((wide, hidden), BF16),
            jax.ShapeDtypeStruct((wide, hidden), BF16),
        ),
        in_specs=[
            pl.BlockSpec(memory_space=pltpu.HBM),
            pl.BlockSpec(memory_space=pltpu.HBM),
            pl.BlockSpec(memory_space=pltpu.HBM),
            pl.BlockSpec(memory_space=pltpu.HBM),
            pl.BlockSpec(memory_space=pltpu.HBM),
            pl.BlockSpec(memory_space=pltpu.HBM),
        ],
        out_specs=[pl.BlockSpec(memory_space=pl.ANY)] * 4,
        scratch_shapes=[
            vmem((1, count), jnp.int32),
            vmem((1, count), F32),
            vmem((wide, hidden), BF16),
            vmem((wide, hidden), BF16),
            vmem((wide, hidden), BF16),
            vmem((hidden, wide), BF16),
            vmem((hidden, wide), BF16),
            vmem((count, wide), BF16),
            vmem((count, wide), BF16),
            vmem((2, 3, 2, 8, count), F32),
            vmem((2, 3, CAP, count), BF16),
            vmem((2, 2, CAP, wide), BF16),
            vmem((2, 3, 2, CAP, wide), BF16),
            vmem((2, 3, units, 2 * hidden), F32),
            vmem((2, 3, units, 2 * hidden), BF16),
            vmem((2, 3, units, 2 * hidden), BF16),
            vmem((2, 3, units, hidden), BF16),
            vmem((2, 3, units, wide), BF16),
            vmem((2, 3, units, wide), BF16),
            vmem((2, 3, units, wide), BF16),
            vmem((2, 3, 2, CAP, 128), F32),
            vmem((2, 3, units, hidden), F32),
            vmem((2, 3, units, hidden), BF16),
            vmem((2, 3, units, hidden), BF16),
            vmem((2, 3, units, 2 * hidden), BF16),
            vmem((2, 3, 2, CAP, wide), BF16),
            vmem((2, 3, CAP, wide), BF16),
            vmem((2, 3, CAP, wide), BF16),
            vmem((count, wide), BF16),
            vmem((3, wide, hidden), BF16),
            dma((6,)),
            dma, dma, dma, dma,
            dma((2, 2)), dma((2, 2)), dma((2, 2)), dma((2, 2)),
            dma((2, 3)), dma((2, 3)), dma((2, 3)), dma((2, 3)),
            dma((2, 3)), dma((2, 3)), dma((2, 3)), dma((2, 3)),
            dma((2, 3)), dma((2, 3)), dma((2, 3)), dma((2, 3)),
            dma((2, 2)), dma((2, 2)),
            dma, dma,
            dma,
            dma((3, GRAD_PARTS)),
            pltpu.SemaphoreType.REGULAR,
            pltpu.SemaphoreType.REGULAR,
        ],
        compiler_params=pltpu.CompilerParams(
            collective_id=0, has_side_effects=True, vmem_limit_bytes=46 << 20
        ),
    )(
        in_hbm(tokens),
        in_hbm(route_dir.reshape(1, count)),
        in_hbm(gate_probs.reshape(1, count)),
        in_hbm(gate_weight[0]),
        in_hbm(up_weight[0]),
        in_hbm(down_weight[0]),
    )
    d_tokens, grad_gate, grad_up, grad_down = settled(outs)
    return d_tokens, grad_gate[None], grad_up[None], grad_down[None]


def solution(mesh):
    return jax.shard_map(
        functools.partial(per_device, mesh.shape["blk"]),
        mesh=mesh,
        in_specs=(
            P(("blk", "dp"), None),
            P(("blk", "dp"), None),
            P(("blk", "dp"), None),
            P("blk", "dp", None),
            P("blk", "dp", None),
            P("blk", "dp", None),
        ),
        out_specs=(
            P(("blk", "dp"), None),
            P("blk", "dp", None),
            P("blk", "dp", None),
            P("blk", "dp", None),
        ),
        check_vma=False,
    )
```
